32 devices in a mesh: row: 4 (over x, core), col: 8 (over z, y).
Axes of the slice: x: 2, y: 2, z: 4, core: 2. Of those that a mesh axis runs over, the one named last changes fastest.
Arguments:
- fiber_rows: bfloat16 [16384, 1024], P(('row', 'col')), may hold values from -6 to 6
- fiber_i: int32 [16384], P(('row', 'col')), may hold values from 0 to 4095
- fiber_j: int32 [16384], P(('row', 'col')), may hold values from 0 to 65535, as said below
- fiber_count: int32 [32], P(('row', 'col')), may hold values from 256 to 512, as said below
- factor_two: bfloat16 [65536, 32], P('col'), may hold values from -1 to 1
Outputs:
- mode_one: bfloat16 [4096, 32768], P(('row', 'col'))
The draws below stay inside these ranges and needn't reach their ends.
Inputs may be any that keep to these rules, and one draw needn't show every extreme that they name: fiber_j of a slot on the device with index c along col lies in c * 8192 to (c + 1) * 8192 - 1. `fiber_count`: among the live slots of one device at most 32 have fiber_i in the block of 128 indices of one device (block fiber_i // 128, in the order row then col); some device is full and reaches 32 for each block it sends to.
All inputs are finite; a program needn't handle non-finite values.
Results may differ from the reference program's by a relative error of at most 0.001.
Values may be sent and summed in bfloat16 or wider, within the bound.
A program may use at most 128 MiB of HBM per device.

```python
import jax
import jax.numpy as jnp
from jax import lax

R = 32
RR = 1024
FIB_DEV = 512
I_DEV = 128
J_COL = 8192
FIBERS = 16384
I1 = 4096
I2 = 65536
N_ROW = 4
N_COL = 8


def fiber_layout(key):
    devices = N_ROW * N_COL
    base = jax.random.fold_in(key, 7)
    key_perm, key_sigma, key_count, key_full = jax.random.split(base, 4)
    perms = jax.vmap(lambda k: jax.random.permutation(k, FIB_DEV))(jax.random.split(key_perm, devices))
    sigmas = jax.vmap(lambda k: jax.random.permutation(k, devices))(jax.random.split(key_sigma, devices))
    bucket = (perms % (devices // 2)).astype(jnp.int32)
    targets = jnp.take_along_axis(sigmas, bucket, axis=1).astype(jnp.int32)
    counts = jax.random.randint(key_count, (devices,), FIB_DEV // 2, FIB_DEV + 1).astype(jnp.int32)
    full = jax.random.randint(key_full, (), 0, devices)
    counts = jnp.where(jnp.arange(devices) == full, FIB_DEV, counts).astype(jnp.int32)
    return (targets, counts)


def draw_fiber_i(key, part):
    devices = N_ROW * N_COL
    targets, counts = fiber_layout(key)
    offsets = jax.random.randint(jax.random.fold_in(key, 11), (devices, FIB_DEV), 0, I_DEV)
    return (targets * I_DEV + offsets).astype(jnp.int32).reshape(FIBERS)


def draw_fiber_j(key, part):
    devices = N_ROW * N_COL
    column = (jnp.arange(devices, dtype=jnp.int32) % N_COL)[:, None]
    offsets = jax.random.randint(jax.random.fold_in(key, 13), (devices, FIB_DEV), 0, J_COL)
    return (column * J_COL + offsets).astype(jnp.int32).reshape(FIBERS)


def draw_fiber_count(key, part):
    targets, counts = fiber_layout(key)
    return counts


def block_levels(rng, extent, shards, smallest, largest):
    def one(dim, shards_of):
        heights = jax.random.uniform(jax.random.fold_in(jax.random.fold_in(rng, 6), dim), (shards_of,), jnp.float32, smallest / len(shards), largest / len(shards))
        return jnp.repeat(jnp.exp(heights), extent[dim] // shards_of).reshape((-1,) + (1,) * (len(extent) - dim - 1))

    level = one(*shards[0])
    for cut in shards[1:]:
        level = level * one(*cut)
    return level


def bell_draw(rng, shape, deviation, reach, cuts=(), held_as=jnp.bfloat16):
    factor_of = block_levels(rng, shape, cuts, -0.22, 0.18) if cuts else 1.0
    values = jax.random.normal(rng, shape, jnp.float32) * deviation * factor_of
    return jnp.minimum(jnp.maximum(values, -reach), reach).astype(held_as)


def setup_inputs(seed: int = 0) -> dict:
    seeds = jax.random.split(jax.random.key(seed), 6)
    return {
        "fiber_rows": bell_draw(seeds[0], (FIBERS, RR), 1.0, 6.0, ((0, 32),)),
        "fiber_i": draw_fiber_i(jax.random.fold_in(seeds[5], 71), 0),
        "fiber_j": draw_fiber_j(jax.random.fold_in(seeds[5], 71), 0),
        "fiber_count": draw_fiber_count(jax.random.fold_in(seeds[5], 71), 0),
        "factor_two": bell_draw(seeds[4], (I2, R), 0.15, 1.0, ((0, 8),)),
    }


def reference(fiber_rows, fiber_i, fiber_j, fiber_count, factor_two):
    slot_ids = jnp.arange(FIBERS, dtype=jnp.int32)
    owners = slot_ids // FIB_DEV
    live = (slot_ids % FIB_DEV) < fiber_count[owners]
    target = jnp.where(live, fiber_i, I1).astype(jnp.int32)
    factor_rows = factor_two[fiber_j]
    block = min(512, FIBERS)
    nblocks = FIBERS // block
    rows_blocks = fiber_rows.reshape(nblocks, block, RR)
    factor_blocks = factor_rows.reshape(nblocks, block, R)
    target_blocks = target.reshape(nblocks, block)

    def accumulate(total, pieces):
        rows, factors, targets = pieces
        outer = factors.astype(jnp.float32)[:, :, None] * rows.astype(jnp.float32)[:, None, :]
        total = total.at[targets].add(outer.reshape(block, R * RR), mode="drop")
        return total, None

    start = jnp.zeros((I1, R * RR), jnp.float32)
    total, _ = lax.scan(accumulate, start, (rows_blocks, factor_blocks, target_blocks))
    return total.astype(jnp.bfloat16)
```

```python
import functools

import jax
import jax.numpy as jnp
from jax import lax
from jax.experimental import pallas as pl
from jax.experimental.pallas import tpu as pltpu
from jax.sharding import PartitionSpec as P

I_DEV = 128
LANES = 128
SUBLANES = 8
KBLOCK = 256
GROUPS = 4
LATE = GROUPS - 1
MESH = pl.DeviceIdType.MESH
ORDER = (2, 1, 0)
ARRIVAL = (0, 1, 2)


def log2(x):
    return x.bit_length() - 1


def one_hot(mask):
    return mask.astype(jnp.float32).astype(jnp.bfloat16)


def contract_lanes(a, b):
    return lax.dot_general(a, b, (((1,), (1,)), ((), ())), preferred_element_type=jnp.float32)


def flip(z, g):
    out = 0
    bit = 1
    while bit < GROUPS:
        out = out + bit * ((z // bit + g // bit) % 2)
        bit *= 2
    return out


def assign_slots(n, cap, count, index):
    stored = index.shape[1]
    live = lax.broadcasted_iota(jnp.int32, (1, stored), 1) < count
    target = jnp.where(live, jnp.right_shift(index, log2(I_DEV)), -1)
    member = lax.broadcasted_iota(jnp.int32, (n, stored), 0) == target
    earlier = lax.broadcasted_iota(jnp.int32, (stored, stored), 0) < lax.broadcasted_iota(
        jnp.int32, (stored, stored), 1
    )
    before = jnp.dot(one_hot(member), one_hot(earlier), preferred_element_type=jnp.float32)
    position = jnp.sum(jnp.where(member, before, 0.0), axis=0, keepdims=True).astype(jnp.int32)
    return target, position


def look_up(local_j, factor_ref):
    rank, col_rows = factor_ref.shape
    stored = local_j.shape[1]
    high = jnp.right_shift(local_j, log2(KBLOCK))
    low = jnp.bitwise_and(local_j, KBLOCK - 1)
    chosen = one_hot(lax.broadcasted_iota(jnp.int32, (KBLOCK, stored), 0) == low)
    pieces = col_rows // KBLOCK
    stacked = jnp.concatenate(
        [factor_ref[:, k * KBLOCK : (k + 1) * KBLOCK] for k in range(pieces)], axis=0
    )
    looked = jnp.dot(stacked, chosen, preferred_element_type=jnp.float32)
    own = jnp.zeros((rank, stored), jnp.float32)
    for k in range(pieces):
        own = own + jnp.where(high == k, looked[k * rank : (k + 1) * rank], 0.0)
    return own


def expand(rank, cap, meta, place, factor_ref, select_ref):
    members = meta.shape[0]
    pack = LANES // cap
    q = rank // pack
    span = members * cap
    for p in range(pack):
        factor_ref[p * q : (p + 1) * q, :] = jnp.concatenate(
            [
                meta[m].astype(jnp.float32)[:q, p * cap : (p + 1) * cap]
                for m in range(members)
            ],
            axis=1,
        )
    row = jnp.concatenate([place[m][:, :cap] for m in range(members)], axis=1)
    select_ref[...] = one_hot(lax.broadcasted_iota(jnp.int32, (I_DEV, span), 0) == row)


def spread_factors(select, factor_ref, first, count):
    return jnp.concatenate(
        [
            select * factor_ref[pl.ds(first + b, 1), :].astype(jnp.bfloat16)
            for b in range(count)
        ],
        axis=0,
    )


def exchange_kernel(
    nrow,
    ncol,
    bounds,
    count_ref,
    i_hbm,
    j_hbm,
    fiber_hbm,
    factor_hbm,
    done_ref,
    late_ref,
    late_rows_ref,
    factor_ref,
    select_ref,
    i_ref,
    j_ref,
    fiber_ref,
    own_factor_ref,
    rows_ref,
    meta_ref,
    place_ref,
    rrows_ref,
    rmeta_ref,
    rplace_ref,
    total_ref,
    send_sem,
    recv_sem,
    own_sem,
    in_sem,
):
    n = nrow * ncol
    members, cap, width = rows_ref.shape[1:]
    per = ncol // GROUPS
    parts = len(bounds) - 1
    rank = factor_ref.shape[0]
    stored = fiber_ref.shape[0]
    r = lax.axis_index("row")
    c = lax.axis_index("col")
    me = r * ncol + c
    z, y = c // per, c % per
    seat = r * per + y

    ready = (
        pltpu.make_async_copy(i_hbm, i_ref, in_sem.at[0]),
        pltpu.make_async_copy(fiber_hbm, fiber_ref, in_sem.at[1]),
        pltpu.make_async_copy(j_hbm, j_ref, in_sem.at[2]),
        pltpu.make_async_copy(factor_hbm, own_factor_ref, in_sem.at[3]),
    )
    for copy in ready:
        copy.start()

    barrier = pltpu.get_barrier_semaphore()

    def greet(k, _):
        other = (me + k) % n
        pl.semaphore_signal(
            barrier, inc=1, device_id=(other // ncol, other % ncol), device_id_type=MESH
        )
        return 0

    lax.fori_loop(1, n, greet, 0)

    def partner(g, k):
        return (r + k // per) % nrow, flip(z, g), (y + k % per) % per

    def remote(g, k, source, dest, row):
        tr, tz, ty = partner(g, k)
        return pltpu.make_async_remote_copy(
            src_ref=source(tr * per + ty),
            dst_ref=dest(seat),
            send_sem=send_sem.at[row, k],
            recv_sem=recv_sem.at[row, k],
            device_id=(tr, tz * per + ty),
            device_id_type=MESH,
        )

    def details(g, k):
        return (
            remote(g, k, lambda t: meta_ref.at[g, t], lambda t: rmeta_ref.at[g, t], g),
            remote(
                g, k, lambda t: place_ref.at[g, t], lambda t: rplace_ref.at[g, t], GROUPS + g
            ),
        )

    def whole(g, k):
        return (
            remote(
                g, k, lambda t: rows_ref.at[g, t], lambda t: rrows_ref.at[g, t], 2 * GROUPS + g
            ),
        )

    def part(p, k):
        columns = pl.ds(bounds[p], bounds[p + 1] - bounds[p])
        return (
            remote(
                LATE,
                k,
                lambda t: rows_ref.at[LATE, t, :, columns],
                lambda t: rrows_ref.at[LATE, t, :, columns],
                2 * GROUPS + LATE + p,
            ),
        )

    def each(first, copies, act):
        def step(k, _):
            for copy in copies(k):
                act(copy)
            return 0

        lax.fori_loop(first, members, step, 0)

    def start(copy):
        copy.start()

    own = (
        pltpu.make_async_copy(rows_ref.at[0, seat], rrows_ref.at[0, seat], own_sem.at[0]),
        pltpu.make_async_copy(meta_ref.at[0, seat], rmeta_ref.at[0, seat], own_sem.at[1]),
        pltpu.make_async_copy(place_ref.at[0, seat], rplace_ref.at[0, seat], own_sem.at[2]),
    )

    ready[0].wait()
    index = i_ref[...]
    target, position = assign_slots(n, cap, count_ref[0], index)
    tcol = jnp.bitwise_and(target, ncol - 1)
    trow = jnp.right_shift(target, log2(ncol))
    tz = jnp.right_shift(tcol, log2(per))
    inner = (trow * per + jnp.bitwise_and(tcol, per - 1)) * cap + position
    inner = jnp.where(target < 0, -1, inner)

    def move_of(g):
        slot = jnp.where(tz == flip(z, g), inner, -1)
        return one_hot(lax.broadcasted_iota(jnp.int32, (members * cap, stored), 0) == slot)

    def pack_rows(g):
        moved = jnp.dot(move_of(g), fiber_ref[...], preferred_element_type=jnp.float32)
        rows_ref[g] = moved.astype(jnp.bfloat16).reshape(members, cap, width)

    ready[1].wait()
    pack_rows(ORDER[0])
    pl.semaphore_wait(barrier, n - 1)
    each(0, functools.partial(whole, ORDER[0]), start)

    ready[2].wait()
    ready[3].wait()
    looked = look_up(j_ref[...] - c * own_factor_ref.shape[1], own_factor_ref)
    local_i = jnp.bitwise_and(index, I_DEV - 1).astype(jnp.float32)
    table = jnp.concatenate(
        [looked, jnp.broadcast_to(local_i, (2 * SUBLANES, stored))], axis=0
    ).astype(jnp.bfloat16)
    pack = LANES // cap
    q = rank // pack
    for g in range(GROUPS):
        spread = contract_lanes(table, move_of(g))
        for m in range(members):
            mine = slice(m * cap, (m + 1) * cap)
            piece = jnp.concatenate(
                [spread[p * q : (p + 1) * q, mine] for p in range(pack)], axis=1
            )
            if q < SUBLANES:
                piece = jnp.concatenate(
                    [piece, jnp.zeros((SUBLANES - q, LANES), jnp.float32)], axis=0
                )
            meta_ref[g, m] = piece.astype(jnp.bfloat16)
            place_ref[g, m] = jnp.concatenate(
                [
                    spread[rank : rank + 1, mine].astype(jnp.int32),
                    jnp.zeros((1, LANES - cap), jnp.int32),
                ],
                axis=1,
            )
    for g in ORDER[1:]:
        pack_rows(g)
        each(1 if g == 0 else 0, functools.partial(whole, g), start)
    for copy in own:
        copy.start()
    for g in ORDER + (LATE,):
        each(1 if g == 0 else 0, functools.partial(details, g), start)
    pack_rows(LATE)
    for p in range(parts):
        each(0, functools.partial(part, p), start)

    per_step = 8
    span_m = per_step * I_DEV
    kgroup = members * cap

    def rows_of(s):
        return pl.ds(pl.multiple_of(s * span_m, span_m), span_m)

    def arrived(copy):
        copy.wait_recv()

    for order, g in enumerate(ARRIVAL):
        first = 1 if g == 0 else 0
        each(first, functools.partial(whole, g), arrived)
        each(first, functools.partial(details, g), arrived)
        if g == 0:
            for copy in own:
                copy.wait()
        expand(rank, cap, rmeta_ref[g], rplace_ref[g], factor_ref, select_ref)

        def multiply(s, _, g=g, order=order):
            left = spread_factors(select_ref[...], factor_ref, s * per_step, per_step)
            product = jnp.dot(
                left, rrows_ref[g].reshape(kgroup, width), preferred_element_type=jnp.float32
            )
            if order > 0:
                product = product + total_ref[rows_of(s), :]
            total_ref[rows_of(s), :] = product
            return 0

        lax.fori_loop(0, rank // per_step, multiply, 0)

    late_ref[...] = total_ref[:, bounds[-2] :]
    def sent(copy):
        copy.wait_send()

    for g in ORDER:
        each(1 if g == 0 else 0, functools.partial(whole, g), sent)
    for g in range(GROUPS):
        each(1 if g == 0 else 0, functools.partial(details, g), sent)
    each(0, functools.partial(details, LATE), arrived)
    expand(rank, cap, rmeta_ref[LATE], rplace_ref[LATE], factor_ref, select_ref)
    for p in range(parts - 1):
        each(0, functools.partial(part, p), arrived)
        low, high = bounds[p], bounds[p + 1]

        def finish(s, _, low=low, high=high):
            left = spread_factors(select_ref[...], factor_ref, s * per_step, per_step)
            product = jnp.dot(
                left,
                rrows_ref[LATE, :, :, low:high].reshape(kgroup, high - low),
                preferred_element_type=jnp.float32,
            )
            product = (product + total_ref[rows_of(s), low:high]).astype(jnp.bfloat16)
            for b in range(per_step):
                at = pl.multiple_of((s * per_step + b) * width + low, LANES)
                done_ref[:, pl.ds(at, high - low)] = product[b * I_DEV : (b + 1) * I_DEV]
            return 0

        lax.fori_loop(0, rank // per_step, finish, 0)

    for p in range(parts - 1):
        each(0, functools.partial(part, p), sent)
    each(0, functools.partial(part, parts - 1), arrived)
    late_rows_ref[...] = rrows_ref[LATE, :, :, bounds[-2] :].reshape(late_rows_ref.shape)

    for p in range(parts-1,parts):
        each(0, functools.partial(part, p), sent)


def finish_kernel(
    width, done_ref, late_ref, rows_ref, factor_ref, select_ref, out_ref, stage_ref, sem
):
    rank = factor_ref.shape[0]
    late = rows_ref.shape[1]
    early = width - late
    per = 8

    def bulk(b):
        columns = pl.ds(pl.multiple_of(b * width, width), early)
        return pltpu.make_async_copy(done_ref.at[:, columns], out_ref.at[:, columns], sem.at[0, b])

    def rest(b):
        columns = pl.ds(pl.multiple_of(b * width + early, LANES), late)
        return pltpu.make_async_copy(stage_ref.at[b], out_ref.at[:, columns], sem.at[1, b])

    def each(act):
        def step(b, _):
            act(b)
            return 0

        lax.fori_loop(0, rank, step, 0)

    each(lambda b: bulk(b).start())
    for s in range(rank // per):
        left = spread_factors(select_ref[...], factor_ref, s * per, per)
        product = jnp.dot(left, rows_ref[...], preferred_element_type=jnp.float32)
        product = product + late_ref[s * per * I_DEV : (s + 1) * per * I_DEV, :]
        for b in range(per):
            stage_ref[s * per + b] = product[b * I_DEV : (b + 1) * I_DEV].astype(jnp.bfloat16)
            rest(s * per + b).start()
    each(lambda b: bulk(b).wait())
    each(lambda b: rest(b).wait())


def body(nrow, ncol, fiber_rows, fiber_i, fiber_j, fiber_count, factor_two):
    n = nrow * ncol
    stored, width = fiber_rows.shape
    col_rows, rank = factor_two.shape
    cap = 2 * stored // n
    members = n // GROUPS
    kgroup = members * cap
    bounds = (0, width // 2, width - LANES, width)
    parts = len(bounds) - 1
    late = bounds[-1] - bounds[-2]
    in_vmem = pl.BlockSpec(memory_space=pltpu.VMEM)
    rows_shape = (GROUPS, members, cap, width)
    meta_shape = (GROUPS, members, SUBLANES, LANES)
    place_shape = (GROUPS, members, 1, LANES)
    sems = 3 * GROUPS + parts - 1
    passed = pl.pallas_call(
        functools.partial(exchange_kernel, nrow, ncol, bounds),
        out_shape=(
            jax.ShapeDtypeStruct((I_DEV, rank * width), jnp.bfloat16),
            jax.ShapeDtypeStruct((I_DEV * rank, late), jnp.float32),
            jax.ShapeDtypeStruct((kgroup, late), jnp.bfloat16),
            jax.ShapeDtypeStruct((rank, kgroup), jnp.float32),
            jax.ShapeDtypeStruct((I_DEV, kgroup), jnp.bfloat16),
        ),
        in_specs=[pl.BlockSpec(memory_space=pltpu.SMEM)] + [pl.BlockSpec(memory_space=pltpu.HBM)] * 4,
        out_specs=(in_vmem,) * 5,
        scratch_shapes=[
            pltpu.VMEM((1, stored), jnp.int32),
            pltpu.VMEM((1, stored), jnp.int32),
            pltpu.VMEM((stored, width), jnp.bfloat16),
            pltpu.VMEM((rank, col_rows), jnp.bfloat16),
            pltpu.VMEM(rows_shape, jnp.bfloat16),
            pltpu.VMEM(meta_shape, jnp.bfloat16),
            pltpu.VMEM(place_shape, jnp.int32),
            pltpu.VMEM(rows_shape, jnp.bfloat16),
            pltpu.VMEM(meta_shape, jnp.bfloat16),
            pltpu.VMEM(place_shape, jnp.int32),
            pltpu.VMEM((I_DEV * rank, width), jnp.float32),
            pltpu.SemaphoreType.DMA((sems, members)),
            pltpu.SemaphoreType.DMA((sems, members)),
            pltpu.SemaphoreType.DMA((3,)),
            pltpu.SemaphoreType.DMA((4,)),
        ],
        compiler_params=pltpu.CompilerParams(
            collective_id=0, has_side_effects=True, vmem_limit_bytes=40 * 1024 * 1024
        ),
        name="exchange",
    )(
        fiber_count,
        *(
            pltpu.with_memory_space_constraint(x, pltpu.HBM)
            for x in (
                fiber_i.reshape(1, stored),
                fiber_j.reshape(1, stored),
                fiber_rows,
                factor_two.T,
            )
        ),
    )
    return pl.pallas_call(
        functools.partial(finish_kernel, width),
        out_shape=jax.ShapeDtypeStruct((I_DEV, rank * width), jnp.bfloat16),
        in_specs=[in_vmem] * 5,
        out_specs=pl.BlockSpec(memory_space=pl.ANY),
        scratch_shapes=[
            pltpu.VMEM((rank, I_DEV, late), jnp.bfloat16),
            pltpu.SemaphoreType.DMA((2, rank)),
        ],
        compiler_params=pltpu.CompilerParams(vmem_limit_bytes=16 * 1024 * 1024),
        name="finish",
    )(*passed)


def solution(mesh):
    in_specs = (
        P(("row", "col"), None),
        P(("row", "col")),
        P(("row", "col")),
        P(("row", "col")),
        P("col", None),
    )
    out_specs = P(("row", "col"), None)
    step = functools.partial(body, mesh.shape["row"], mesh.shape["col"])
    return jax.shard_map(step, mesh=mesh, in_specs=in_specs, out_specs=out_specs, check_vma=False)
```

```python
import functools

import jax
import jax.numpy as jnp
from jax import lax
from jax.experimental import pallas as pl
from jax.experimental.pallas import tpu as pltpu
from jax.sharding import PartitionSpec as P

I_DEV = 128
LANES = 128
SUBLANES = 8
KBLOCK = 256
GROUPS = 4
LATE = GROUPS - 1
MESH = pl.DeviceIdType.MESH
ORDER = (2, 1, 0)
ARRIVAL = (0, 1, 2)


def log2(x):
    return x.bit_length() - 1


def one_hot(mask):
    return mask.astype(jnp.float32).astype(jnp.bfloat16)


def contract_lanes(a, b):
    return lax.dot_general(a, b, (((1,), (1,)), ((), ())), preferred_element_type=jnp.float32)


def flip(z, g):
    out = 0
    bit = 1
    while bit < GROUPS:
        out = out + bit * ((z // bit + g // bit) % 2)
        bit *= 2
    return out


def assign_slots(n, cap, count, index):
    stored = index.shape[1]
    live = lax.broadcasted_iota(jnp.int32, (1, stored), 1) < count
    target = jnp.where(live, jnp.right_shift(index, log2(I_DEV)), -1)
    member = lax.broadcasted_iota(jnp.int32, (n, stored), 0) == target
    earlier = lax.broadcasted_iota(jnp.int32, (stored, stored), 0) < lax.broadcasted_iota(
        jnp.int32, (stored, stored), 1
    )
    before = jnp.dot(one_hot(member), one_hot(earlier), preferred_element_type=jnp.float32)
    position = jnp.sum(jnp.where(member, before, 0.0), axis=0, keepdims=True).astype(jnp.int32)
    return target, position


def look_up(local_j, factor_ref):
    rank, col_rows = factor_ref.shape
    stored = local_j.shape[1]
    high = jnp.right_shift(local_j, log2(KBLOCK))
    low = jnp.bitwise_and(local_j, KBLOCK - 1)
    chosen = one_hot(lax.broadcasted_iota(jnp.int32, (KBLOCK, stored), 0) == low)
    pieces = col_rows // KBLOCK
    stacked = jnp.concatenate(
        [factor_ref[:, k * KBLOCK : (k + 1) * KBLOCK] for k in range(pieces)], axis=0
    )
    looked = jnp.dot(stacked, chosen, preferred_element_type=jnp.float32)
    own = jnp.zeros((rank, stored), jnp.float32)
    for k in range(pieces):
        own = own + jnp.where(high == k, looked[k * rank : (k + 1) * rank], 0.0)
    return own


def expand(rank, cap, meta, place, factor_ref, select_ref):
    members = meta.shape[0]
    pack = LANES // cap
    q = rank // pack
    span = members * cap
    for p in range(pack):
        factor_ref[p * q : (p + 1) * q, :] = jnp.concatenate(
            [
                meta[m].astype(jnp.float32)[:q, p * cap : (p + 1) * cap]
                for m in range(members)
            ],
            axis=1,
        )
    row = jnp.concatenate([place[m][:, :cap] for m in range(members)], axis=1)
    select_ref[...] = one_hot(lax.broadcasted_iota(jnp.int32, (I_DEV, span), 0) == row)


def spread_factors(select, factor_ref, first, count):
    return jnp.concatenate(
        [
            select * factor_ref[pl.ds(first + b, 1), :].astype(jnp.bfloat16)
            for b in range(count)
        ],
        axis=0,
    )


def exchange_kernel(
    nrow,
    ncol,
    bounds,
    count_ref,
    i_hbm,
    j_hbm,
    fiber_hbm,
    factor_hbm,
    done_ref,
    late_ref,
    late_rows_ref,
    factor_ref,
    select_ref,
    i_ref,
    j_ref,
    fiber_ref,
    own_factor_ref,
    rows_ref,
    meta_ref,
    place_ref,
    rrows_ref,
    rmeta_ref,
    rplace_ref,
    total_ref,
    send_sem,
    recv_sem,
    own_sem,
    in_sem,
):
    n = nrow * ncol
    members, cap, width = rows_ref.shape[1:]
    per = ncol // GROUPS
    parts = len(bounds) - 1
    rank = factor_ref.shape[0]
    stored = fiber_ref.shape[0]
    r = lax.axis_index("row")
    c = lax.axis_index("col")
    me = r * ncol + c
    z, y = c // per, c % per
    seat = r * per + y

    ready = (
        pltpu.make_async_copy(i_hbm, i_ref, in_sem.at[0]),
        pltpu.make_async_copy(fiber_hbm, fiber_ref, in_sem.at[1]),
        pltpu.make_async_copy(j_hbm, j_ref, in_sem.at[2]),
        pltpu.make_async_copy(factor_hbm, own_factor_ref, in_sem.at[3]),
    )
    for copy in ready:
        copy.start()

    barrier = pltpu.get_barrier_semaphore()

    def greet(k, _):
        other = (me + k) % n
        pl.semaphore_signal(
            barrier, inc=1, device_id=(other // ncol, other % ncol), device_id_type=MESH
        )
        return 0

    lax.fori_loop(1, n, greet, 0)

    def partner(g, k):
        return (r + k // per) % nrow, flip(z, g), (y + k % per) % per

    def remote(g, k, source, dest, row):
        tr, tz, ty = partner(g, k)
        return pltpu.make_async_remote_copy(
            src_ref=source(tr * per + ty),
            dst_ref=dest(seat),
            send_sem=send_sem.at[row, k],
            recv_sem=recv_sem.at[row, k],
            device_id=(tr, tz * per + ty),
            device_id_type=MESH,
        )

    def details(g, k):
        return (
            remote(g, k, lambda t: meta_ref.at[g, t], lambda t: rmeta_ref.at[g, t], g),
            remote(
                g, k, lambda t: place_ref.at[g, t], lambda t: rplace_ref.at[g, t], GROUPS + g
            ),
        )

    def whole(g, k):
        return (
            remote(
                g, k, lambda t: rows_ref.at[g, t], lambda t: rrows_ref.at[g, t], 2 * GROUPS + g
            ),
        )

    def part(p, k):
        columns = pl.ds(bounds[p], bounds[p + 1] - bounds[p])
        return (
            remote(
                LATE,
                k,
                lambda t: rows_ref.at[LATE, t, :, columns],
                lambda t: rrows_ref.at[LATE, t, :, columns],
                2 * GROUPS + LATE + p,
            ),
        )

    def each(first, copies, act, last=members):
        def step(k, _):
            for copy in copies(k):
                act(copy)
            return 0

        lax.fori_loop(first, last, step, 0)

    def start(copy):
        copy.start()

    own = (
        pltpu.make_async_copy(rows_ref.at[0, seat], rrows_ref.at[0, seat], own_sem.at[0]),
        pltpu.make_async_copy(meta_ref.at[0, seat], rmeta_ref.at[0, seat], own_sem.at[1]),
        pltpu.make_async_copy(place_ref.at[0, seat], rplace_ref.at[0, seat], own_sem.at[2]),
    )

    ready[0].wait()
    index = i_ref[...]
    target, position = assign_slots(n, cap, count_ref[0], index)
    tcol = jnp.bitwise_and(target, ncol - 1)
    trow = jnp.right_shift(target, log2(ncol))
    tz = jnp.right_shift(tcol, log2(per))
    inner = (trow * per + jnp.bitwise_and(tcol, per - 1)) * cap + position
    inner = jnp.where(target < 0, -1, inner)

    def move_of(g):
        slot = jnp.where(tz == flip(z, g), inner, -1)
        return one_hot(lax.broadcasted_iota(jnp.int32, (members * cap, stored), 0) == slot)

    def pack_rows(g):
        moved = jnp.dot(move_of(g), fiber_ref[...], preferred_element_type=jnp.float32)
        rows_ref[g] = moved.astype(jnp.bfloat16).reshape(members, cap, width)

    ready[1].wait()
    pack_rows(ORDER[0])
    pl.semaphore_wait(barrier, n - 1)
    each(0, functools.partial(whole, ORDER[0]), start, members // 2)
    for g in ORDER[1:]:
        pack_rows(g)
        each(1 if g == 0 else 0, functools.partial(whole, g), start)
    each(members // 2, functools.partial(whole, ORDER[0]), start)

    ready[2].wait()
    ready[3].wait()
    looked = look_up(j_ref[...] - c * own_factor_ref.shape[1], own_factor_ref)
    local_i = jnp.bitwise_and(index, I_DEV - 1).astype(jnp.float32)
    table = jnp.concatenate(
        [looked, jnp.broadcast_to(local_i, (2 * SUBLANES, stored))], axis=0
    ).astype(jnp.bfloat16)
    pack = LANES // cap
    q = rank // pack
    for g in range(GROUPS):
        spread = contract_lanes(table, move_of(g))
        for m in range(members):
            mine = slice(m * cap, (m + 1) * cap)
            piece = jnp.concatenate(
                [spread[p * q : (p + 1) * q, mine] for p in range(pack)], axis=1
            )
            if q < SUBLANES:
                piece = jnp.concatenate(
                    [piece, jnp.zeros((SUBLANES - q, LANES), jnp.float32)], axis=0
                )
            meta_ref[g, m] = piece.astype(jnp.bfloat16)
            place_ref[g, m] = jnp.concatenate(
                [
                    spread[rank : rank + 1, mine].astype(jnp.int32),
                    jnp.zeros((1, LANES - cap), jnp.int32),
                ],
                axis=1,
            )
    for copy in own:
        copy.start()
    for g in ORDER + (LATE,):
        each(1 if g == 0 else 0, functools.partial(details, g), start)
    pack_rows(LATE)
    for p in range(parts):
        each(0, functools.partial(part, p), start)

    per_step = 8
    span_m = per_step * I_DEV
    kgroup = members * cap

    def rows_of(s):
        return pl.ds(pl.multiple_of(s * span_m, span_m), span_m)

    def arrived(copy):
        copy.wait_recv()

    for order, g in enumerate(ARRIVAL):
        first = 1 if g == 0 else 0
        each(first, functools.partial(whole, g), arrived)
        each(first, functools.partial(details, g), arrived)
        if g == 0:
            for copy in own:
                copy.wait()
        expand(rank, cap, rmeta_ref[g], rplace_ref[g], factor_ref, select_ref)

        def multiply(s, _, g=g, order=order):
            left = spread_factors(select_ref[...], factor_ref, s * per_step, per_step)
            product = jnp.dot(
                left, rrows_ref[g].reshape(kgroup, width), preferred_element_type=jnp.float32
            )
            for part_ref, low, high in (
                (total_ref, 0, bounds[-2]),
                (late_ref, bounds[-2], bounds[-1]),
            ):
                term = product[:, low:high]
                if order > 0:
                    term = term + part_ref[rows_of(s), :]
                part_ref[rows_of(s), :] = term
            return 0

        lax.fori_loop(0, rank // per_step, multiply, 0)

    def sent(copy):
        copy.wait_send()

    for g in ORDER:
        each(1 if g == 0 else 0, functools.partial(whole, g), sent)
    for g in range(GROUPS):
        each(1 if g == 0 else 0, functools.partial(details, g), sent)
    each(0, functools.partial(details, LATE), arrived)
    expand(rank, cap, rmeta_ref[LATE], rplace_ref[LATE], factor_ref, select_ref)
    for p in range(parts - 1):
        each(0, functools.partial(part, p), arrived)
        low, high = bounds[p], bounds[p + 1]

        def finish(s, _, low=low, high=high):
            left = spread_factors(select_ref[...], factor_ref, s * per_step, per_step)
            product = jnp.dot(
                left,
                rrows_ref[LATE, :, :, low:high].reshape(kgroup, high - low),
                preferred_element_type=jnp.float32,
            )
            product = (product + total_ref[rows_of(s), low:high]).astype(jnp.bfloat16)
            for b in range(per_step):
                at = pl.multiple_of((s * per_step + b) * width + low, LANES)
                done_ref[:, pl.ds(at, high - low)] = product[b * I_DEV : (b + 1) * I_DEV]
            return 0

        lax.fori_loop(0, rank // per_step, finish, 0)

    for p in range(parts - 1):
        each(0, functools.partial(part, p), sent)
    each(0, functools.partial(part, parts - 1), arrived)
    late_rows_ref[...] = rrows_ref[LATE, :, :, bounds[-2] :].reshape(late_rows_ref.shape)

    for p in range(parts-1,parts):
        each(0, functools.partial(part, p), sent)


def finish_kernel(
    width, done_ref, late_ref, rows_ref, factor_ref, select_ref, out_ref, stage_ref, sem
):
    rank = factor_ref.shape[0]
    late = rows_ref.shape[1]
    early = width - late
    per = 4

    def bulk(b):
        columns = pl.ds(pl.multiple_of(b * width, width), early)
        return pltpu.make_async_copy(done_ref.at[:, columns], out_ref.at[:, columns], sem.at[0, b])

    def rest(b):
        columns = pl.ds(pl.multiple_of(b * width + early, LANES), late)
        return pltpu.make_async_copy(stage_ref.at[b], out_ref.at[:, columns], sem.at[1, b])

    def each(act):
        def step(b, _):
            act(b)
            return 0

        lax.fori_loop(0, rank, step, 0)

    each(lambda b: bulk(b).start())

    def multiply(s, _):
        left = spread_factors(select_ref[...], factor_ref, s * per, per)
        product = jnp.dot(left, rows_ref[...], preferred_element_type=jnp.float32)
        span_m = per * I_DEV
        product = product + late_ref[pl.ds(pl.multiple_of(s * span_m, span_m), span_m), :]
        for b in range(per):
            stage_ref[s * per + b] = product[b * I_DEV : (b + 1) * I_DEV].astype(jnp.bfloat16)
            rest(s * per + b).start()
        return 0

    lax.fori_loop(0, rank // per, multiply, 0)
    each(lambda b: bulk(b).wait())
    each(lambda b: rest(b).wait())


def body(nrow, ncol, fiber_rows, fiber_i, fiber_j, fiber_count, factor_two):
    n = nrow * ncol
    stored, width = fiber_rows.shape
    col_rows, rank = factor_two.shape
    cap = 2 * stored // n
    members = n // GROUPS
    kgroup = members * cap
    bounds = (0, width * 3 // 4, width)
    parts = len(bounds) - 1
    late = bounds[-1] - bounds[-2]
    in_vmem = pl.BlockSpec(memory_space=pltpu.VMEM)
    rows_shape = (GROUPS, members, cap, width)
    meta_shape = (GROUPS, members, SUBLANES, LANES)
    place_shape = (GROUPS, members, 1, LANES)
    sems = 3 * GROUPS + parts - 1
    passed = pl.pallas_call(
        functools.partial(exchange_kernel, nrow, ncol, bounds),
        out_shape=(
            jax.ShapeDtypeStruct((I_DEV, rank * width), jnp.bfloat16),
            jax.ShapeDtypeStruct((I_DEV * rank, late), jnp.float32),
            jax.ShapeDtypeStruct((kgroup, late), jnp.bfloat16),
            jax.ShapeDtypeStruct((rank, kgroup), jnp.float32),
            jax.ShapeDtypeStruct((I_DEV, kgroup), jnp.bfloat16),
        ),
        in_specs=[pl.BlockSpec(memory_space=pltpu.SMEM)] + [pl.BlockSpec(memory_space=pltpu.HBM)] * 4,
        out_specs=(in_vmem,) * 5,
        scratch_shapes=[
            pltpu.VMEM((1, stored), jnp.int32),
            pltpu.VMEM((1, stored), jnp.int32),
            pltpu.VMEM((stored, width), jnp.bfloat16),
            pltpu.VMEM((rank, col_rows), jnp.bfloat16),
            pltpu.VMEM(rows_shape, jnp.bfloat16),
            pltpu.VMEM(meta_shape, jnp.bfloat16),
            pltpu.VMEM(place_shape, jnp.int32),
            pltpu.VMEM(rows_shape, jnp.bfloat16),
            pltpu.VMEM(meta_shape, jnp.bfloat16),
            pltpu.VMEM(place_shape, jnp.int32),
            pltpu.VMEM((I_DEV * rank, width - late), jnp.float32),
            pltpu.SemaphoreType.DMA((sems, members)),
            pltpu.SemaphoreType.DMA((sems, members)),
            pltpu.SemaphoreType.DMA((3,)),
            pltpu.SemaphoreType.DMA((4,)),
        ],
        compiler_params=pltpu.CompilerParams(
            collective_id=0, has_side_effects=True, vmem_limit_bytes=40 * 1024 * 1024
        ),
        name="exchange",
    )(
        fiber_count,
        *(
            pltpu.with_memory_space_constraint(x, pltpu.HBM)
            for x in (
                fiber_i.reshape(1, stored),
                fiber_j.reshape(1, stored),
                fiber_rows,
                factor_two.T,
            )
        ),
    )
    return pl.pallas_call(
        functools.partial(finish_kernel, width),
        out_shape=jax.ShapeDtypeStruct((I_DEV, rank * width), jnp.bfloat16),
        in_specs=[in_vmem] * 5,
        out_specs=pl.BlockSpec(memory_space=pl.ANY),
        scratch_shapes=[
            pltpu.VMEM((rank, I_DEV, late), jnp.bfloat16),
            pltpu.SemaphoreType.DMA((2, rank)),
        ],
        compiler_params=pltpu.CompilerParams(vmem_limit_bytes=16 * 1024 * 1024),
        name="finish",
    )(*passed)


def solution(mesh):
    in_specs = (
        P(("row", "col"), None),
        P(("row", "col")),
        P(("row", "col")),
        P(("row", "col")),
        P("col", None),
    )
    out_specs = P(("row", "col"), None)
    step = functools.partial(body, mesh.shape["row"], mesh.shape["col"])
    return jax.shard_map(step, mesh=mesh, in_specs=in_specs, out_specs=out_specs, check_vma=False)
```

```python
import functools

import jax
import jax.numpy as jnp
from jax import lax
from jax.experimental import pallas as pl
from jax.experimental.pallas import tpu as pltpu
from jax.sharding import PartitionSpec as P

I_DEV = 128
LANES = 128
SUBLANES = 8
KBLOCK = 256
GROUPS = 4
LATE = GROUPS - 1
MESH = pl.DeviceIdType.MESH
ORDER = (2, 1, 0)
ARRIVAL = (0, 1, 2)


def log2(x):
    return x.bit_length() - 1


def one_hot(mask):
    return mask.astype(jnp.float32).astype(jnp.bfloat16)


def contract_lanes(a, b):
    return lax.dot_general(a, b, (((1,), (1,)), ((), ())), preferred_element_type=jnp.float32)


def flip(a, b, size):
    out = 0
    bit = 1
    while bit < size:
        out = out + bit * ((a // bit + b // bit) % 2)
        bit *= 2
    return out


def assign_slots(n, cap, count, index):
    stored = index.shape[1]
    live = lax.broadcasted_iota(jnp.int32, (1, stored), 1) < count
    target = jnp.where(live, jnp.right_shift(index, log2(I_DEV)), -1)
    member = lax.broadcasted_iota(jnp.int32, (n, stored), 0) == target
    earlier = lax.broadcasted_iota(jnp.int32, (stored, stored), 0) < lax.broadcasted_iota(
        jnp.int32, (stored, stored), 1
    )
    before = jnp.dot(one_hot(member), one_hot(earlier), preferred_element_type=jnp.float32)
    position = jnp.sum(jnp.where(member, before, 0.0), axis=0, keepdims=True).astype(jnp.int32)
    return target, position


def look_up(local_j, factor_ref):
    rank, col_rows = factor_ref.shape
    stored = local_j.shape[1]
    high = jnp.right_shift(local_j, log2(KBLOCK))
    low = jnp.bitwise_and(local_j, KBLOCK - 1)
    chosen = one_hot(lax.broadcasted_iota(jnp.int32, (KBLOCK, stored), 0) == low)
    pieces = col_rows // KBLOCK
    stacked = jnp.concatenate(
        [factor_ref[:, k * KBLOCK : (k + 1) * KBLOCK] for k in range(pieces)], axis=0
    )
    looked = jnp.dot(stacked, chosen, preferred_element_type=jnp.float32)
    own = jnp.zeros((rank, stored), jnp.float32)
    for k in range(pieces):
        own = own + jnp.where(high == k, looked[k * rank : (k + 1) * rank], 0.0)
    return own


def expand(rank, cap, meta_ref, factor_ref, select_ref):
    members, blocks = meta_ref.shape[:2]
    pack = LANES // cap
    q = rank // pack
    span = members * cap
    held = [
        jnp.concatenate([meta_ref[m, i].astype(jnp.float32) for i in range(blocks - 1)], axis=0)
        for m in range(members)
    ]
    for p in range(pack):
        factor_ref[p * q : (p + 1) * q, :] = jnp.concatenate(
            [block[:q, p * cap : (p + 1) * cap] for block in held], axis=1
        )
    row = jnp.concatenate(
        [meta_ref[m, blocks - 1].astype(jnp.float32)[:1, :cap] for m in range(members)], axis=1
    )
    select_ref[...] = one_hot(
        lax.broadcasted_iota(jnp.int32, (I_DEV, span), 0) == row.astype(jnp.int32)
    )


def spread_factors(select, factor_ref, first, count):
    return jnp.concatenate(
        [
            select * factor_ref[pl.ds(first + b, 1), :].astype(jnp.bfloat16)
            for b in range(count)
        ],
        axis=0,
    )


def exchange_kernel(
    nrow,
    ncol,
    bounds,
    count_ref,
    i_hbm,
    j_hbm,
    fiber_hbm,
    factor_hbm,
    done_ref,
    late_ref,
    late_rows_ref,
    factor_ref,
    select_ref,
    i_ref,
    j_ref,
    fiber_ref,
    own_factor_ref,
    rows_ref,
    meta_ref,
    rrows_ref,
    rmeta_ref,
    total_ref,
    send_sem,
    recv_sem,
    own_sem,
    in_sem,
    known_sem,
):
    n = nrow * ncol
    members, cap, width = rows_ref.shape[1:]
    per = ncol // GROUPS
    parts = len(bounds) - 1
    rank = factor_ref.shape[0]
    stored = fiber_ref.shape[0]
    r = lax.axis_index("row")
    c = lax.axis_index("col")
    z, y = c // per, c % per
    seat = r * per + y

    ready = (
        pltpu.make_async_copy(i_hbm, i_ref, in_sem.at[0]),
        pltpu.make_async_copy(fiber_hbm, fiber_ref, in_sem.at[1]),
        pltpu.make_async_copy(j_hbm, j_ref, in_sem.at[2]),
        pltpu.make_async_copy(factor_hbm, own_factor_ref, in_sem.at[3]),
    )
    for copy in ready:
        copy.start()

    sides = [(flip(r, 1 << b, nrow), c) for b in range(log2(nrow))]
    sides += [(r, z * per + flip(y, 1 << b, per)) for b in range(log2(per))]
    low_z = (r, flip(z, 1, GROUPS) * per + y)
    high_z = (r, flip(z, 2, GROUPS) * per + y)
    neighbours = [high_z] + sides + [low_z]
    barrier = pltpu.get_barrier_semaphore()
    for other in neighbours:
        pl.semaphore_signal(barrier, inc=1, device_id=other, device_id_type=MESH)

    def tell(d):
        other = (sides + [low_z])[d]
        pl.semaphore_signal(known_sem.at[d], inc=1, device_id=other, device_id_type=MESH)

    def hear(d):
        pl.semaphore_wait(known_sem.at[d], 1)

    def partner(g, k):
        return flip(r, k % nrow, nrow), flip(z, g, GROUPS), flip(y, k // nrow, per)

    def remote(g, k, source, dest, row):
        tr, tz, ty = partner(g, k)
        return pltpu.make_async_remote_copy(
            src_ref=source(tr * per + ty),
            dst_ref=dest(seat),
            send_sem=send_sem.at[row, k],
            recv_sem=recv_sem.at[row, k],
            device_id=(tr, tz * per + ty),
            device_id_type=MESH,
        )

    def details(g, k):
        return (
            remote(g, k, lambda t: meta_ref.at[g, t], lambda t: rmeta_ref.at[g, t], g),
        )

    def whole(g, k):
        return (
            remote(
                g, k, lambda t: rows_ref.at[g, t], lambda t: rrows_ref.at[g, t], 2 * GROUPS + g
            ),
        )

    def part(p, k):
        columns = pl.ds(bounds[p], bounds[p + 1] - bounds[p])
        return (
            remote(
                LATE,
                k,
                lambda t: rows_ref.at[LATE, t, :, columns],
                lambda t: rrows_ref.at[LATE, t, :, columns],
                2 * GROUPS + LATE + p,
            ),
        )

    def each(first, copies, act, last=members):
        def step(k, _):
            for copy in copies(k):
                act(copy)
            return 0

        lax.fori_loop(first, last, step, 0)

    def start(copy):
        copy.start()

    own = (
        pltpu.make_async_copy(rows_ref.at[0, seat], rrows_ref.at[0, seat], own_sem.at[0]),
        pltpu.make_async_copy(meta_ref.at[0, seat], rmeta_ref.at[0, seat], own_sem.at[1]),
    )

    ready[0].wait()
    index = i_ref[...]
    target, position = assign_slots(n, cap, count_ref[0], index)
    tcol = jnp.bitwise_and(target, ncol - 1)
    trow = jnp.right_shift(target, log2(ncol))
    tz = jnp.right_shift(tcol, log2(per))
    inner = (trow * per + jnp.bitwise_and(tcol, per - 1)) * cap + position
    inner = jnp.where(target < 0, -1, inner)

    def move_of(g):
        slot = jnp.where(tz == flip(z, g, GROUPS), inner, -1)
        return one_hot(lax.broadcasted_iota(jnp.int32, (members * cap, stored), 0) == slot)

    def pack_rows(g):
        moved = jnp.dot(move_of(g), fiber_ref[...], preferred_element_type=jnp.float32)
        rows_ref[g] = moved.astype(jnp.bfloat16).reshape(members, cap, width)

    ready[1].wait()
    pack_rows(ORDER[0])
    half = members // 2
    pl.semaphore_wait(barrier, len(neighbours))
    tell(0)
    each(0, functools.partial(whole, ORDER[0]), start, 1)
    for d in range(len(sides) - 1):
        hear(d)
        tell(d + 1)
        each(1 << d, functools.partial(whole, ORDER[0]), start, 2 << d)
    pack_rows(ORDER[1])
    hear(len(sides) - 1)
    tell(len(sides))
    pack_rows(ORDER[2])
    hear(len(sides))
    for g in ORDER[1:]:
        each(1 if g == 0 else 0, functools.partial(whole, g), start)
    each(half, functools.partial(whole, ORDER[0]), start)

    ready[2].wait()
    ready[3].wait()
    looked = look_up(j_ref[...] - c * own_factor_ref.shape[1], own_factor_ref)
    local_i = jnp.bitwise_and(index, I_DEV - 1).astype(jnp.float32)
    table = jnp.concatenate(
        [looked, jnp.broadcast_to(local_i, (2 * SUBLANES, stored))], axis=0
    ).astype(jnp.bfloat16)
    pack = LANES // cap
    q = rank // pack
    for g in range(GROUPS):
        spread = contract_lanes(table, move_of(g))
        for m in range(members):
            mine = slice(m * cap, (m + 1) * cap)
            piece = jnp.concatenate(
                [spread[p * q : (p + 1) * q, mine] for p in range(pack)], axis=1
            )
            if q < SUBLANES:
                piece = jnp.concatenate(
                    [piece, jnp.zeros((SUBLANES - q, LANES), jnp.float32)], axis=0
                )
            place = jnp.concatenate(
                [spread[rank : rank + 2, mine], jnp.zeros((2, LANES - cap), jnp.float32)], axis=1
            )
            for i in range(SUBLANES // 2):
                meta_ref[g, m, i] = piece[2 * i : 2 * i + 2].astype(jnp.bfloat16)
            meta_ref[g, m, SUBLANES // 2] = place.astype(jnp.bfloat16)
    for copy in own:
        copy.start()
    for g in ORDER + (LATE,):
        each(1 if g == 0 else 0, functools.partial(details, g), start)
    pack_rows(LATE)
    for p in range(parts):
        each(0, functools.partial(part, p), start)

    per_step = 8
    span_m = per_step * I_DEV
    kgroup = members * cap

    def rows_of(s):
        return pl.ds(pl.multiple_of(s * span_m, span_m), span_m)

    def arrived(copy):
        copy.wait_recv()

    for order, g in enumerate(ARRIVAL):
        first = 1 if g == 0 else 0
        each(first, functools.partial(whole, g), arrived)
        each(first, functools.partial(details, g), arrived)
        if g == 0:
            for copy in own:
                copy.wait()
        expand(rank, cap, rmeta_ref.at[g], factor_ref, select_ref)

        def multiply(s, _, g=g, order=order):
            left = spread_factors(select_ref[...], factor_ref, s * per_step, per_step)
            product = jnp.dot(
                left, rrows_ref[g].reshape(kgroup, width), preferred_element_type=jnp.float32
            )
            for part_ref, low, high in (
                (total_ref, 0, bounds[-2]),
                (late_ref, bounds[-2], bounds[-1]),
            ):
                term = product[:, low:high]
                if order > 0:
                    term = term + part_ref[rows_of(s), :]
                part_ref[rows_of(s), :] = term
            return 0

        lax.fori_loop(0, rank // per_step, multiply, 0)

    def sent(copy):
        copy.wait_send()

    for g in ORDER:
        each(1 if g == 0 else 0, functools.partial(whole, g), sent)
    for g in range(GROUPS):
        each(1 if g == 0 else 0, functools.partial(details, g), sent)
    each(0, functools.partial(details, LATE), arrived)
    expand(rank, cap, rmeta_ref.at[LATE], factor_ref, select_ref)
    for p in range(parts - 1):
        each(0, functools.partial(part, p), arrived)
        low, high = bounds[p], bounds[p + 1]

        def finish(s, _, low=low, high=high):
            left = spread_factors(select_ref[...], factor_ref, s * per_step, per_step)
            product = jnp.dot(
                left,
                rrows_ref[LATE, :, :, low:high].reshape(kgroup, high - low),
                preferred_element_type=jnp.float32,
            )
            product = (product + total_ref[rows_of(s), low:high]).astype(jnp.bfloat16)
            for b in range(per_step):
                at = pl.multiple_of((s * per_step + b) * width + low, LANES)
                done_ref[:, pl.ds(at, high - low)] = product[b * I_DEV : (b + 1) * I_DEV]
            return 0

        lax.fori_loop(0, rank // per_step, finish, 0)

    for p in range(parts - 1):
        each(0, functools.partial(part, p), sent)
    each(0, functools.partial(part, parts - 1), arrived)
    late_rows_ref[...] = rrows_ref[LATE, :, :, bounds[-2] :].reshape(late_rows_ref.shape)

    for p in range(parts-1,parts):
        each(0, functools.partial(part, p), sent)


def finish_kernel(
    width, done_ref, late_ref, rows_ref, factor_ref, select_ref, out_ref, stage_ref, sem
):
    rank = factor_ref.shape[0]
    late = rows_ref.shape[1]
    early = width - late
    per = 4

    def bulk(b):
        columns = pl.ds(pl.multiple_of(b * width, width), early)
        return pltpu.make_async_copy(done_ref.at[:, columns], out_ref.at[:, columns], sem.at[0, b])

    def rest(b):
        columns = pl.ds(pl.multiple_of(b * width + early, LANES), late)
        return pltpu.make_async_copy(stage_ref.at[b], out_ref.at[:, columns], sem.at[1, b])

    def each(act):
        def step(b, _):
            act(b)
            return 0

        lax.fori_loop(0, rank, step, 0)

    each(lambda b: bulk(b).start())

    def multiply(s, _):
        left = spread_factors(select_ref[...], factor_ref, s * per, per)
        product = jnp.dot(left, rows_ref[...], preferred_element_type=jnp.float32)
        span_m = per * I_DEV
        product = product + late_ref[pl.ds(pl.multiple_of(s * span_m, span_m), span_m), :]
        for b in range(per):
            stage_ref[s * per + b] = product[b * I_DEV : (b + 1) * I_DEV].astype(jnp.bfloat16)
            rest(s * per + b).start()
        return 0

    lax.fori_loop(0, rank // per, multiply, 0)
    each(lambda b: bulk(b).wait())
    each(lambda b: rest(b).wait())


def body(nrow, ncol, fiber_rows, fiber_i, fiber_j, fiber_count, factor_two):
    n = nrow * ncol
    stored, width = fiber_rows.shape
    col_rows, rank = factor_two.shape
    cap = 2 * stored // n
    members = n // GROUPS
    kgroup = members * cap
    bounds = (0, width * 3 // 4, width)
    parts = len(bounds) - 1
    late = bounds[-1] - bounds[-2]
    in_vmem = pl.BlockSpec(memory_space=pltpu.VMEM)
    rows_shape = (GROUPS, members, cap, width)
    meta_shape = (GROUPS, members, SUBLANES // 2 + 1, 2, LANES)
    sems = 3 * GROUPS + parts - 1
    passed = pl.pallas_call(
        functools.partial(exchange_kernel, nrow, ncol, bounds),
        out_shape=(
            jax.ShapeDtypeStruct((I_DEV, rank * width), jnp.bfloat16),
            jax.ShapeDtypeStruct((I_DEV * rank, late), jnp.float32),
            jax.ShapeDtypeStruct((kgroup, late), jnp.bfloat16),
            jax.ShapeDtypeStruct((rank, kgroup), jnp.float32),
            jax.ShapeDtypeStruct((I_DEV, kgroup), jnp.bfloat16),
        ),
        in_specs=[pl.BlockSpec(memory_space=pltpu.SMEM)] + [pl.BlockSpec(memory_space=pltpu.HBM)] * 4,
        out_specs=(in_vmem,) * 5,
        scratch_shapes=[
            pltpu.VMEM((1, stored), jnp.int32),
            pltpu.VMEM((1, stored), jnp.int32),
            pltpu.VMEM((stored, width), jnp.bfloat16),
            pltpu.VMEM((rank, col_rows), jnp.bfloat16),
            pltpu.VMEM(rows_shape, jnp.bfloat16),
            pltpu.VMEM(meta_shape, jnp.bfloat16),
            pltpu.VMEM(rows_shape, jnp.bfloat16),
            pltpu.VMEM(meta_shape, jnp.bfloat16),
            pltpu.VMEM((I_DEV * rank, width - late), jnp.float32),
            pltpu.SemaphoreType.DMA((sems, members)),
            pltpu.SemaphoreType.DMA((sems, members)),
            pltpu.SemaphoreType.DMA((3,)),
            pltpu.SemaphoreType.DMA((4,)),
            pltpu.SemaphoreType.REGULAR((log2(n) - 1,)),
        ],
        compiler_params=pltpu.CompilerParams(
            collective_id=0, has_side_effects=True, vmem_limit_bytes=40 * 1024 * 1024
        ),
        name="exchange",
    )(
        fiber_count,
        *(
            pltpu.with_memory_space_constraint(x, pltpu.HBM)
            for x in (
                fiber_i.reshape(1, stored),
                fiber_j.reshape(1, stored),
                fiber_rows,
                factor_two.T,
            )
        ),
    )
    return pl.pallas_call(
        functools.partial(finish_kernel, width),
        out_shape=jax.ShapeDtypeStruct((I_DEV, rank * width), jnp.bfloat16),
        in_specs=[in_vmem] * 5,
        out_specs=pl.BlockSpec(memory_space=pl.ANY),
        scratch_shapes=[
            pltpu.VMEM((rank, I_DEV, late), jnp.bfloat16),
            pltpu.SemaphoreType.DMA((2, rank)),
        ],
        compiler_params=pltpu.CompilerParams(vmem_limit_bytes=16 * 1024 * 1024),
        name="finish",
    )(*passed)


def solution(mesh):
    in_specs = (
        P(("row", "col"), None),
        P(("row", "col")),
        P(("row", "col")),
        P(("row", "col")),
        P("col", None),
    )
    out_specs = P(("row", "col"), None)
    step = functools.partial(body, mesh.shape["row"], mesh.shape["col"])
    return jax.shard_map(step, mesh=mesh, in_specs=in_specs, out_specs=out_specs, check_vma=False)
```

```python
import functools

import jax
import jax.numpy as jnp
from jax import lax
from jax.experimental import pallas as pl
from jax.experimental.pallas import tpu as pltpu
from jax.sharding import PartitionSpec as P

I_DEV = 128
LANES = 128
SUBLANES = 8
KBLOCK = 256
GROUPS = 4
LATE = GROUPS - 1
MESH = pl.DeviceIdType.MESH
ORDER = (2, 1, 0)
ARRIVAL = (0, 1, 2)


def log2(x):
    return x.bit_length() - 1


def one_hot(mask):
    return mask.astype(jnp.float32).astype(jnp.bfloat16)


def contract_lanes(a, b):
    return lax.dot_general(a, b, (((1,), (1,)), ((), ())), preferred_element_type=jnp.float32)


def flip(a, b, size):
    out = 0
    bit = 1
    while bit < size:
        out = out + bit * ((a // bit + b // bit) % 2)
        bit *= 2
    return out


def assign_slots(n, cap, count, index):
    stored = index.shape[1]
    live = lax.broadcasted_iota(jnp.int32, (1, stored), 1) < count
    target = jnp.where(live, jnp.right_shift(index, log2(I_DEV)), -1)
    member = lax.broadcasted_iota(jnp.int32, (n, stored), 0) == target
    earlier = lax.broadcasted_iota(jnp.int32, (stored, stored), 0) < lax.broadcasted_iota(
        jnp.int32, (stored, stored), 1
    )
    before = jnp.dot(one_hot(member), one_hot(earlier), preferred_element_type=jnp.float32)
    position = jnp.sum(jnp.where(member, before, 0.0), axis=0, keepdims=True).astype(jnp.int32)
    return target, position


def look_up(local_j, factor_ref):
    rank, col_rows = factor_ref.shape
    stored = local_j.shape[1]
    high = jnp.right_shift(local_j, log2(KBLOCK))
    low = jnp.bitwise_and(local_j, KBLOCK - 1)
    chosen = one_hot(lax.broadcasted_iota(jnp.int32, (KBLOCK, stored), 0) == low)
    pieces = col_rows // KBLOCK
    stacked = jnp.concatenate(
        [factor_ref[:, k * KBLOCK : (k + 1) * KBLOCK] for k in range(pieces)], axis=0
    )
    looked = jnp.dot(stacked, chosen, preferred_element_type=jnp.float32)
    own = jnp.zeros((rank, stored), jnp.float32)
    for k in range(pieces):
        own = own + jnp.where(high == k, looked[k * rank : (k + 1) * rank], 0.0)
    return own


def expand(rank, cap, meta_ref, factor_ref, select_ref):
    members, blocks = meta_ref.shape[:2]
    pack = LANES // cap
    q = rank // pack
    span = members * cap
    held = [
        jnp.concatenate([meta_ref[m, i].astype(jnp.float32) for i in range(blocks - 1)], axis=0)
        for m in range(members)
    ]
    for p in range(pack):
        factor_ref[p * q : (p + 1) * q, :] = jnp.concatenate(
            [block[:q, p * cap : (p + 1) * cap] for block in held], axis=1
        )
    row = jnp.concatenate(
        [meta_ref[m, blocks - 1].astype(jnp.float32)[:1, :cap] for m in range(members)], axis=1
    )
    select_ref[...] = one_hot(
        lax.broadcasted_iota(jnp.int32, (I_DEV, span), 0) == row.astype(jnp.int32)
    )


def spread_factors(select, factor_ref, first, count):
    return jnp.concatenate(
        [
            select * factor_ref[pl.ds(first + b, 1), :].astype(jnp.bfloat16)
            for b in range(count)
        ],
        axis=0,
    )


def exchange_kernel(
    nrow,
    ncol,
    bounds,
    count_ref,
    i_hbm,
    j_hbm,
    fiber_hbm,
    factor_hbm,
    done_ref,
    late_ref,
    late_rows_ref,
    factor_ref,
    select_ref,
    i_ref,
    j_ref,
    fiber_ref,
    own_factor_ref,
    rows_ref,
    meta_ref,
    rrows_ref,
    rmeta_ref,
    total_ref,
    send_sem,
    recv_sem,
    own_sem,
    in_sem,
    known_sem,
):
    n = nrow * ncol
    members, cap, width = rows_ref.shape[1:]
    per = ncol // GROUPS
    parts = len(bounds) - 1
    rank = factor_ref.shape[0]
    stored = fiber_ref.shape[0]
    r = lax.axis_index("row")
    c = lax.axis_index("col")
    z, y = c // per, c % per
    seat = r * per + y

    ready = (
        pltpu.make_async_copy(i_hbm, i_ref, in_sem.at[0]),
        pltpu.make_async_copy(fiber_hbm, fiber_ref, in_sem.at[1]),
        pltpu.make_async_copy(j_hbm, j_ref, in_sem.at[2]),
        pltpu.make_async_copy(factor_hbm, own_factor_ref, in_sem.at[3]),
    )
    sides = [(flip(r, 1 << b, nrow), c) for b in range(log2(nrow))]
    sides += [(r, z * per + flip(y, 1 << b, per)) for b in range(log2(per))]
    low_z = (r, flip(z, 1, GROUPS) * per + y)
    high_z = (r, flip(z, 2, GROUPS) * per + y)
    neighbours = [high_z] + sides + [low_z]
    barrier = pltpu.get_barrier_semaphore()
    for other in neighbours:
        pl.semaphore_signal(barrier, inc=1, device_id=other, device_id_type=MESH)
    for copy in ready:
        copy.start()

    def tell(d):
        other = (sides + [low_z])[d]
        pl.semaphore_signal(known_sem.at[d], inc=1, device_id=other, device_id_type=MESH)

    def hear(d):
        pl.semaphore_wait(known_sem.at[d], 1)

    def partner(g, k):
        return flip(r, k % nrow, nrow), flip(z, g, GROUPS), flip(y, k // nrow, per)

    def remote(g, k, source, dest, row):
        tr, tz, ty = partner(g, k)
        return pltpu.make_async_remote_copy(
            src_ref=source(tr * per + ty),
            dst_ref=dest(seat),
            send_sem=send_sem.at[row, k],
            recv_sem=recv_sem.at[row, k],
            device_id=(tr, tz * per + ty),
            device_id_type=MESH,
        )

    def details(g, k):
        return (
            remote(g, k, lambda t: meta_ref.at[g, t], lambda t: rmeta_ref.at[g, t], g),
        )

    def whole(g, k):
        return (
            remote(
                g, k, lambda t: rows_ref.at[g, t], lambda t: rrows_ref.at[g, t], 2 * GROUPS + g
            ),
        )

    def part(p, k):
        columns = pl.ds(bounds[p], bounds[p + 1] - bounds[p])
        return (
            remote(
                LATE,
                k,
                lambda t: rows_ref.at[LATE, t, :, columns],
                lambda t: rrows_ref.at[LATE, t, :, columns],
                2 * GROUPS + LATE + p,
            ),
        )

    def each(first, copies, act, last=members):
        def step(k, _):
            for copy in copies(k):
                act(copy)
            return 0

        lax.fori_loop(first, last, step, 0)

    def start(copy):
        copy.start()

    own = (
        pltpu.make_async_copy(rows_ref.at[0, seat], rrows_ref.at[0, seat], own_sem.at[0]),
        pltpu.make_async_copy(meta_ref.at[0, seat], rmeta_ref.at[0, seat], own_sem.at[1]),
    )

    ready[0].wait()
    index = i_ref[...]
    target, position = assign_slots(n, cap, count_ref[0], index)
    tcol = jnp.bitwise_and(target, ncol - 1)
    trow = jnp.right_shift(target, log2(ncol))
    tz = jnp.right_shift(tcol, log2(per))
    inner = (trow * per + jnp.bitwise_and(tcol, per - 1)) * cap + position
    inner = jnp.where(target < 0, -1, inner)

    def move_of(g):
        slot = jnp.where(tz == flip(z, g, GROUPS), inner, -1)
        return one_hot(lax.broadcasted_iota(jnp.int32, (members * cap, stored), 0) == slot)

    def pack_rows(g):
        moved = jnp.dot(move_of(g), fiber_ref[...], preferred_element_type=jnp.float32)
        rows_ref[g] = moved.astype(jnp.bfloat16).reshape(members, cap, width)

    ready[1].wait()
    pack_rows(ORDER[0])
    half = members // 2
    pl.semaphore_wait(barrier, len(neighbours))
    tell(0)
    each(0, functools.partial(whole, ORDER[0]), start, 1)
    for d in range(len(sides) - 1):
        hear(d)
        tell(d + 1)
        each(1 << d, functools.partial(whole, ORDER[0]), start, 2 << d)
    pack_rows(ORDER[1])
    hear(len(sides) - 1)
    tell(len(sides))
    pack_rows(ORDER[2])
    hear(len(sides))
    for g in ORDER[1:]:
        each(1 if g == 0 else 0, functools.partial(whole, g), start)
    each(half, functools.partial(whole, ORDER[0]), start)

    ready[2].wait()
    ready[3].wait()
    looked = look_up(j_ref[...] - c * own_factor_ref.shape[1], own_factor_ref)
    local_i = jnp.bitwise_and(index, I_DEV - 1).astype(jnp.float32)
    table = jnp.concatenate(
        [looked, jnp.broadcast_to(local_i, (2 * SUBLANES, stored))], axis=0
    ).astype(jnp.bfloat16)
    pack = LANES // cap
    q = rank // pack
    for g in range(GROUPS):
        spread = contract_lanes(table, move_of(g))
        for m in range(members):
            mine = slice(m * cap, (m + 1) * cap)
            piece = jnp.concatenate(
                [spread[p * q : (p + 1) * q, mine] for p in range(pack)], axis=1
            )
            if q < SUBLANES:
                piece = jnp.concatenate(
                    [piece, jnp.zeros((SUBLANES - q, LANES), jnp.float32)], axis=0
                )
            place = jnp.concatenate(
                [spread[rank : rank + 2, mine], jnp.zeros((2, LANES - cap), jnp.float32)], axis=1
            )
            for i in range(SUBLANES // 2):
                meta_ref[g, m, i] = piece[2 * i : 2 * i + 2].astype(jnp.bfloat16)
            meta_ref[g, m, SUBLANES // 2] = place.astype(jnp.bfloat16)
    for copy in own:
        copy.start()
    for g in ORDER + (LATE,):
        each(1 if g == 0 else 0, functools.partial(details, g), start)
    pack_rows(LATE)
    for p in range(parts):
        each(0, functools.partial(part, p), start)

    per_step = 8
    span_m = per_step * I_DEV
    kgroup = members * cap

    def rows_of(s):
        return pl.ds(pl.multiple_of(s * span_m, span_m), span_m)

    def arrived(copy):
        copy.wait_recv()

    for order, g in enumerate(ARRIVAL):
        first = 1 if g == 0 else 0
        each(first, functools.partial(whole, g), arrived)
        each(first, functools.partial(details, g), arrived)
        if g == 0:
            for copy in own:
                copy.wait()
        expand(rank, cap, rmeta_ref.at[g], factor_ref, select_ref)

        def multiply(s, _, g=g, order=order):
            left = spread_factors(select_ref[...], factor_ref, s * per_step, per_step)
            product = jnp.dot(
                left, rrows_ref[g].reshape(kgroup, width), preferred_element_type=jnp.float32
            )
            for part_ref, low, high in (
                (total_ref, 0, bounds[-2]),
                (late_ref, bounds[-2], bounds[-1]),
            ):
                term = product[:, low:high]
                if order > 0:
                    term = term + part_ref[rows_of(s), :]
                part_ref[rows_of(s), :] = term
            return 0

        lax.fori_loop(0, rank // per_step, multiply, 0)

    def sent(copy):
        copy.wait_send()

    for g in ORDER:
        each(1 if g == 0 else 0, functools.partial(whole, g), sent)
    for g in range(GROUPS):
        each(1 if g == 0 else 0, functools.partial(details, g), sent)
    each(0, functools.partial(details, LATE), arrived)
    expand(rank, cap, rmeta_ref.at[LATE], factor_ref, select_ref)
    for p in range(parts - 1):
        each(0, functools.partial(part, p), arrived)
        low, high = bounds[p], bounds[p + 1]

        def finish(s, _, low=low, high=high):
            left = spread_factors(select_ref[...], factor_ref, s * per_step, per_step)
            product = jnp.dot(
                left,
                rrows_ref[LATE, :, :, low:high].reshape(kgroup, high - low),
                preferred_element_type=jnp.float32,
            )
            product = (product + total_ref[rows_of(s), low:high]).astype(jnp.bfloat16)
            for b in range(per_step):
                at = pl.multiple_of((s * per_step + b) * width + low, LANES)
                done_ref[:, pl.ds(at, high - low)] = product[b * I_DEV : (b + 1) * I_DEV]
            return 0

        lax.fori_loop(0, rank // per_step, finish, 0)

    for p in range(parts - 1):
        each(0, functools.partial(part, p), sent)
    each(0, functools.partial(part, parts - 1), arrived)
    late_rows_ref[...] = rrows_ref[LATE, :, :, bounds[-2] :].reshape(late_rows_ref.shape)

    for p in range(parts-1,parts):
        each(0, functools.partial(part, p), sent)


def finish_kernel(
    width, done_ref, late_ref, rows_ref, factor_ref, select_ref, out_ref, stage_ref, sem
):
    rank = factor_ref.shape[0]
    late = rows_ref.shape[1]
    early = width - late
    per = 4

    def bulk(b):
        columns = pl.ds(pl.multiple_of(b * width, width), early)
        return pltpu.make_async_copy(done_ref.at[:, columns], out_ref.at[:, columns], sem.at[0, b])

    def rest(b):
        columns = pl.ds(pl.multiple_of(b * width + early, LANES), late)
        return pltpu.make_async_copy(stage_ref.at[b], out_ref.at[:, columns], sem.at[1, b])

    def each(act):
        def step(b, _):
            act(b)
            return 0

        lax.fori_loop(0, rank, step, 0)

    each(lambda b: bulk(b).start())

    def multiply(s, _):
        left = spread_factors(select_ref[...], factor_ref, s * per, per)
        product = jnp.dot(left, rows_ref[...], preferred_element_type=jnp.float32)
        span_m = per * I_DEV
        product = product + late_ref[pl.ds(pl.multiple_of(s * span_m, span_m), span_m), :]
        for b in range(per):
            stage_ref[s * per + b] = product[b * I_DEV : (b + 1) * I_DEV].astype(jnp.bfloat16)
            rest(s * per + b).start()
        return 0

    lax.fori_loop(0, rank // per, multiply, 0)
    each(lambda b: bulk(b).wait())
    each(lambda b: rest(b).wait())


def body(nrow, ncol, fiber_rows, fiber_i, fiber_j, fiber_count, factor_two):
    n = nrow * ncol
    stored, width = fiber_rows.shape
    col_rows, rank = factor_two.shape
    cap = 2 * stored // n
    members = n // GROUPS
    kgroup = members * cap
    bounds = (0, width // 2, width)
    parts = len(bounds) - 1
    late = bounds[-1] - bounds[-2]
    in_vmem = pl.BlockSpec(memory_space=pltpu.VMEM)
    rows_shape = (GROUPS, members, cap, width)
    meta_shape = (GROUPS, members, SUBLANES // 2 + 1, 2, LANES)
    sems = 3 * GROUPS + parts - 1
    passed = pl.pallas_call(
        functools.partial(exchange_kernel, nrow, ncol, bounds),
        out_shape=(
            jax.ShapeDtypeStruct((I_DEV, rank * width), jnp.bfloat16),
            jax.ShapeDtypeStruct((I_DEV * rank, late), jnp.float32),
            jax.ShapeDtypeStruct((kgroup, late), jnp.bfloat16),
            jax.ShapeDtypeStruct((rank, kgroup), jnp.float32),
            jax.ShapeDtypeStruct((I_DEV, kgroup), jnp.bfloat16),
        ),
        in_specs=[pl.BlockSpec(memory_space=pltpu.SMEM)] + [pl.BlockSpec(memory_space=pltpu.HBM)] * 4,
        out_specs=(in_vmem,) * 5,
        scratch_shapes=[
            pltpu.VMEM((1, stored), jnp.int32),
            pltpu.VMEM((1, stored), jnp.int32),
            pltpu.VMEM((stored, width), jnp.bfloat16),
            pltpu.VMEM((rank, col_rows), jnp.bfloat16),
            pltpu.VMEM(rows_shape, jnp.bfloat16),
            pltpu.VMEM(meta_shape, jnp.bfloat16),
            pltpu.VMEM(rows_shape, jnp.bfloat16),
            pltpu.VMEM(meta_shape, jnp.bfloat16),
            pltpu.VMEM((I_DEV * rank, width - late), jnp.float32),
            pltpu.SemaphoreType.DMA((sems, members)),
            pltpu.SemaphoreType.DMA((sems, members)),
            pltpu.SemaphoreType.DMA((3,)),
            pltpu.SemaphoreType.DMA((4,)),
            pltpu.SemaphoreType.REGULAR((log2(n) - 1,)),
        ],
        compiler_params=pltpu.CompilerParams(
            collective_id=0, has_side_effects=True, vmem_limit_bytes=24 * 1024 * 1024
        ),
        name="exchange",
    )(
        fiber_count,
        *(
            pltpu.with_memory_space_constraint(x, pltpu.HBM)
            for x in (
                fiber_i.reshape(1, stored),
                fiber_j.reshape(1, stored),
                fiber_rows,
                factor_two.T,
            )
        ),
    )
    return pl.pallas_call(
        functools.partial(finish_kernel, width),
        out_shape=jax.ShapeDtypeStruct((I_DEV, rank * width), jnp.bfloat16),
        in_specs=[in_vmem] * 5,
        out_specs=pl.BlockSpec(memory_space=pl.ANY),
        scratch_shapes=[
            pltpu.VMEM((rank, I_DEV, late), jnp.bfloat16),
            pltpu.SemaphoreType.DMA((2, rank)),
        ],
        compiler_params=pltpu.CompilerParams(vmem_limit_bytes=16 * 1024 * 1024),
        name="finish",
    )(*passed)


def solution(mesh):
    in_specs = (
        P(("row", "col"), None),
        P(("row", "col")),
        P(("row", "col")),
        P(("row", "col")),
        P("col", None),
    )
    out_specs = P(("row", "col"), None)
    step = functools.partial(body, mesh.shape["row"], mesh.shape["col"])
    return jax.shard_map(step, mesh=mesh, in_specs=in_specs, out_specs=out_specs, check_vma=False)
```

```python
import functools

import jax
import jax.numpy as jnp
from jax import lax
from jax.experimental import pallas as pl
from jax.experimental.pallas import tpu as pltpu
from jax.sharding import PartitionSpec as P

I_DEV = 128
LANES = 128
SUBLANES = 8
KBLOCK = 256
GROUPS = 4
LATE = GROUPS - 1
MESH = pl.DeviceIdType.MESH
ORDER = (2, 1, 0)
ARRIVAL = (0, 1, 2)


def log2(x):
    return x.bit_length() - 1


def one_hot(mask):
    return mask.astype(jnp.float32).astype(jnp.bfloat16)


def contract_lanes(a, b):
    return lax.dot_general(a, b, (((1,), (1,)), ((), ())), preferred_element_type=jnp.float32)


def flip(a, b, size):
    out = 0
    bit = 1
    while bit < size:
        out = out + bit * ((a // bit + b // bit) % 2)
        bit *= 2
    return out


def assign_slots(n, cap, count, index):
    stored = index.shape[1]
    live = lax.broadcasted_iota(jnp.int32, (1, stored), 1) < count
    target = jnp.where(live, jnp.right_shift(index, log2(I_DEV)), -1)
    member = lax.broadcasted_iota(jnp.int32, (n, stored), 0) == target
    earlier = lax.broadcasted_iota(jnp.int32, (stored, stored), 0) < lax.broadcasted_iota(
        jnp.int32, (stored, stored), 1
    )
    before = jnp.dot(one_hot(member), one_hot(earlier), preferred_element_type=jnp.float32)
    position = jnp.sum(jnp.where(member, before, 0.0), axis=0, keepdims=True).astype(jnp.int32)
    return target, position


def look_up(local_j, factor_ref):
    rank, col_rows = factor_ref.shape
    stored = local_j.shape[1]
    high = jnp.right_shift(local_j, log2(KBLOCK))
    low = jnp.bitwise_and(local_j, KBLOCK - 1)
    chosen = one_hot(lax.broadcasted_iota(jnp.int32, (KBLOCK, stored), 0) == low)
    pieces = col_rows // KBLOCK
    stacked = jnp.concatenate(
        [factor_ref[:, k * KBLOCK : (k + 1) * KBLOCK] for k in range(pieces)], axis=0
    )
    looked = jnp.dot(stacked, chosen, preferred_element_type=jnp.float32)
    own = jnp.zeros((rank, stored), jnp.float32)
    for k in range(pieces):
        own = own + jnp.where(high == k, looked[k * rank : (k + 1) * rank], 0.0)
    return own


def expand(rank, cap, meta_ref, factor_ref, select_ref):
    members, blocks = meta_ref.shape[:2]
    pack = LANES // cap
    q = rank // pack
    span = members * cap
    held = [
        jnp.concatenate([meta_ref[m, i].astype(jnp.float32) for i in range(blocks - 1)], axis=0)
        for m in range(members)
    ]
    for p in range(pack):
        factor_ref[p * q : (p + 1) * q, :] = jnp.concatenate(
            [block[:q, p * cap : (p + 1) * cap] for block in held], axis=1
        )
    row = jnp.concatenate(
        [meta_ref[m, blocks - 1].astype(jnp.float32)[:1, :cap] for m in range(members)], axis=1
    )
    select_ref[...] = one_hot(
        lax.broadcasted_iota(jnp.int32, (I_DEV, span), 0) == row.astype(jnp.int32)
    )


def spread_factors(select, factor_ref, first, count):
    return jnp.concatenate(
        [
            select * factor_ref[pl.ds(first + b, 1), :].astype(jnp.bfloat16)
            for b in range(count)
        ],
        axis=0,
    )


def exchange_kernel(
    nrow,
    ncol,
    bounds,
    count_ref,
    i_hbm,
    j_hbm,
    fiber_hbm,
    factor_hbm,
    done_ref,
    late_ref,
    late_rows_ref,
    factor_ref,
    select_ref,
    i_ref,
    j_ref,
    fiber_ref,
    own_factor_ref,
    rows_ref,
    meta_ref,
    rrows_ref,
    rmeta_ref,
    total_ref,
    send_sem,
    recv_sem,
    own_sem,
    in_sem,
    known_sem,
):
    n = nrow * ncol
    members, cap, width = rows_ref.shape[1:]
    per = ncol // GROUPS
    parts = len(bounds) - 1
    rank = factor_ref.shape[0]
    stored = fiber_ref.shape[0]
    r = lax.axis_index("row")
    c = lax.axis_index("col")
    z, y = c // per, c % per
    seat = r * per + y

    ready = (
        pltpu.make_async_copy(i_hbm, i_ref, in_sem.at[0]),
        pltpu.make_async_copy(fiber_hbm, fiber_ref, in_sem.at[1]),
        pltpu.make_async_copy(j_hbm, j_ref, in_sem.at[2]),
        pltpu.make_async_copy(factor_hbm, own_factor_ref, in_sem.at[3]),
    )
    sides = [(flip(r, 1 << b, nrow), c) for b in range(log2(nrow))]
    sides += [(r, z * per + flip(y, 1 << b, per)) for b in range(log2(per))]
    low_z = (r, flip(z, 1, GROUPS) * per + y)
    high_z = (r, flip(z, 2, GROUPS) * per + y)
    neighbours = [high_z] + sides + [low_z]
    barrier = pltpu.get_barrier_semaphore()
    for other in neighbours:
        pl.semaphore_signal(barrier, inc=1, device_id=other, device_id_type=MESH)
    for copy in ready:
        copy.start()

    def tell(d):
        other = (sides + [low_z])[d]
        pl.semaphore_signal(known_sem.at[d], inc=1, device_id=other, device_id_type=MESH)

    def hear(d):
        pl.semaphore_wait(known_sem.at[d], 1)

    def partner(g, k):
        return flip(r, k % nrow, nrow), flip(z, g, GROUPS), flip(y, k // nrow, per)

    def remote(g, k, source, dest, row):
        tr, tz, ty = partner(g, k)
        return pltpu.make_async_remote_copy(
            src_ref=source(tr * per + ty),
            dst_ref=dest(seat),
            send_sem=send_sem.at[row, k],
            recv_sem=recv_sem.at[row, k],
            device_id=(tr, tz * per + ty),
            device_id_type=MESH,
        )

    def details(g, k):
        return (
            remote(g, k, lambda t: meta_ref.at[g, t], lambda t: rmeta_ref.at[g, t], g),
        )

    def whole(g, k):
        return (
            remote(
                g, k, lambda t: rows_ref.at[g, t], lambda t: rrows_ref.at[g, t], 2 * GROUPS + g
            ),
        )

    def part(p, k):
        columns = pl.ds(bounds[p], bounds[p + 1] - bounds[p])
        return (
            remote(
                LATE,
                k,
                lambda t: rows_ref.at[LATE, t, :, columns],
                lambda t: rrows_ref.at[LATE, t, :, columns],
                2 * GROUPS + LATE + p,
            ),
        )

    def each(first, copies, act, last=members):
        def step(k, _):
            for copy in copies(k):
                act(copy)
            return 0

        lax.fori_loop(first, last, step, 0)

    def start(copy):
        copy.start()

    own = (
        pltpu.make_async_copy(rows_ref.at[0, seat], rrows_ref.at[0, seat], own_sem.at[0]),
        pltpu.make_async_copy(meta_ref.at[0, seat], rmeta_ref.at[0, seat], own_sem.at[1]),
    )

    ready[0].wait()
    index = i_ref[...]
    target, position = assign_slots(n, cap, count_ref[0], index)
    tcol = jnp.bitwise_and(target, ncol - 1)
    trow = jnp.right_shift(target, log2(ncol))
    tz = jnp.right_shift(tcol, log2(per))
    inner = (trow * per + jnp.bitwise_and(tcol, per - 1)) * cap + position
    inner = jnp.where(target < 0, -1, inner)

    def move_of(g):
        slot = jnp.where(tz == flip(z, g, GROUPS), inner, -1)
        return one_hot(lax.broadcasted_iota(jnp.int32, (members * cap, stored), 0) == slot)

    def pack_rows(g):
        moved = jnp.dot(move_of(g), fiber_ref[...], preferred_element_type=jnp.float32)
        rows_ref[g] = moved.astype(jnp.bfloat16).reshape(members, cap, width)

    ready[1].wait()
    pack_rows(ORDER[0])
    half = members // 2
    pl.semaphore_wait(barrier, len(neighbours))
    tell(0)
    each(0, functools.partial(whole, ORDER[0]), start, 1)
    for d in range(len(sides) - 1):
        hear(d)
        tell(d + 1)
        each(1 << d, functools.partial(whole, ORDER[0]), start, 2 << d)
    pack_rows(ORDER[1])
    hear(len(sides) - 1)
    tell(len(sides))
    pack_rows(ORDER[2])
    hear(len(sides))
    for g in ORDER[1:]:
        each(1 if g == 0 else 0, functools.partial(whole, g), start)
    each(half, functools.partial(whole, ORDER[0]), start)

    ready[2].wait()
    ready[3].wait()
    looked = look_up(j_ref[...] - c * own_factor_ref.shape[1], own_factor_ref)
    local_i = jnp.bitwise_and(index, I_DEV - 1).astype(jnp.float32)
    table = jnp.concatenate(
        [looked, jnp.broadcast_to(local_i, (2 * SUBLANES, stored))], axis=0
    ).astype(jnp.bfloat16)
    pack = LANES // cap
    q = rank // pack
    for g in range(GROUPS):
        spread = contract_lanes(table, move_of(g))
        for m in range(members):
            mine = slice(m * cap, (m + 1) * cap)
            piece = jnp.concatenate(
                [spread[p * q : (p + 1) * q, mine] for p in range(pack)], axis=1
            )
            if q < SUBLANES:
                piece = jnp.concatenate(
                    [piece, jnp.zeros((SUBLANES - q, LANES), jnp.float32)], axis=0
                )
            place = jnp.concatenate(
                [spread[rank : rank + 2, mine], jnp.zeros((2, LANES - cap), jnp.float32)], axis=1
            )
            for i in range(SUBLANES // 2):
                meta_ref[g, m, i] = piece[2 * i : 2 * i + 2].astype(jnp.bfloat16)
            meta_ref[g, m, SUBLANES // 2] = place.astype(jnp.bfloat16)
    for copy in own:
        copy.start()
    for g in ORDER:
        each(1 if g == 0 else 0, functools.partial(details, g), start)
    pack_rows(LATE)
    each(0, functools.partial(part, 0), start)
    each(0, functools.partial(details, LATE), start)
    for p in range(1, parts):
        each(0, functools.partial(part, p), start)

    per_step = 8
    span_m = per_step * I_DEV
    kgroup = members * cap

    def rows_of(s):
        return pl.ds(pl.multiple_of(s * span_m, span_m), span_m)

    def arrived(copy):
        copy.wait_recv()

    for order, g in enumerate(ARRIVAL):
        first = 1 if g == 0 else 0
        each(first, functools.partial(whole, g), arrived)
        each(first, functools.partial(details, g), arrived)
        if g == 0:
            for copy in own:
                copy.wait()
        expand(rank, cap, rmeta_ref.at[g], factor_ref, select_ref)

        def multiply(s, _, g=g, order=order):
            left = spread_factors(select_ref[...], factor_ref, s * per_step, per_step)
            product = jnp.dot(
                left, rrows_ref[g].reshape(kgroup, width), preferred_element_type=jnp.float32
            )
            for part_ref, low, high in (
                (total_ref, 0, bounds[-2]),
                (late_ref, bounds[-2], bounds[-1]),
            ):
                term = product[:, low:high]
                if order > 0:
                    term = term + part_ref[rows_of(s), :]
                part_ref[rows_of(s), :] = term
            return 0

        lax.fori_loop(0, rank // per_step, multiply, 0)

    def sent(copy):
        copy.wait_send()

    for g in ORDER:
        each(1 if g == 0 else 0, functools.partial(whole, g), sent)
    for g in range(GROUPS):
        each(1 if g == 0 else 0, functools.partial(details, g), sent)
    each(0, functools.partial(details, LATE), arrived)
    expand(rank, cap, rmeta_ref.at[LATE], factor_ref, select_ref)
    for p in range(parts - 1):
        each(0, functools.partial(part, p), arrived)
        low, high = bounds[p], bounds[p + 1]

        def finish(s, _, low=low, high=high):
            left = spread_factors(select_ref[...], factor_ref, s * per_step, per_step)
            product = jnp.dot(
                left,
                rrows_ref[LATE, :, :, low:high].reshape(kgroup, high - low),
                preferred_element_type=jnp.float32,
            )
            product = (product + total_ref[rows_of(s), low:high]).astype(jnp.bfloat16)
            for b in range(per_step):
                at = pl.multiple_of((s * per_step + b) * width + low, LANES)
                done_ref[:, pl.ds(at, high - low)] = product[b * I_DEV : (b + 1) * I_DEV]
            return 0

        lax.fori_loop(0, rank // per_step, finish, 0)

    for p in range(parts - 1):
        each(0, functools.partial(part, p), sent)
    each(0, functools.partial(part, parts - 1), arrived)
    late_rows_ref[...] = rrows_ref[LATE, :, :, bounds[-2] :].reshape(late_rows_ref.shape)

    for p in range(parts-1,parts):
        each(0, functools.partial(part, p), sent)


def finish_kernel(
    width, done_ref, late_ref, rows_ref, factor_ref, select_ref, out_ref, stage_ref, sem
):
    rank = factor_ref.shape[0]
    late = rows_ref.shape[1]
    early = width - late
    per = 4

    def bulk(b):
        columns = pl.ds(pl.multiple_of(b * width, width), early)
        return pltpu.make_async_copy(done_ref.at[:, columns], out_ref.at[:, columns], sem.at[0, b])

    def rest(b):
        columns = pl.ds(pl.multiple_of(b * width + early, LANES), late)
        return pltpu.make_async_copy(stage_ref.at[b], out_ref.at[:, columns], sem.at[1, b])

    def each(act):
        def step(b, _):
            act(b)
            return 0

        lax.fori_loop(0, rank, step, 0)

    each(lambda b: bulk(b).start())

    def multiply(s, _):
        left = spread_factors(select_ref[...], factor_ref, s * per, per)
        product = jnp.dot(left, rows_ref[...], preferred_element_type=jnp.float32)
        span_m = per * I_DEV
        product = product + late_ref[pl.ds(pl.multiple_of(s * span_m, span_m), span_m), :]
        for b in range(per):
            stage_ref[s * per + b] = product[b * I_DEV : (b + 1) * I_DEV].astype(jnp.bfloat16)
            rest(s * per + b).start()
        return 0

    lax.fori_loop(0, rank // per, multiply, 0)
    each(lambda b: bulk(b).wait())
    each(lambda b: rest(b).wait())


def body(nrow, ncol, fiber_rows, fiber_i, fiber_j, fiber_count, factor_two):
    n = nrow * ncol
    stored, width = fiber_rows.shape
    col_rows, rank = factor_two.shape
    cap = 2 * stored // n
    members = n // GROUPS
    kgroup = members * cap
    bounds = (0, width // 2, width)
    parts = len(bounds) - 1
    late = bounds[-1] - bounds[-2]
    in_vmem = pl.BlockSpec(memory_space=pltpu.VMEM)
    rows_shape = (GROUPS, members, cap, width)
    meta_shape = (GROUPS, members, SUBLANES // 2 + 1, 2, LANES)
    sems = 3 * GROUPS + parts - 1
    passed = pl.pallas_call(
        functools.partial(exchange_kernel, nrow, ncol, bounds),
        out_shape=(
            jax.ShapeDtypeStruct((I_DEV, rank * width), jnp.bfloat16),
            jax.ShapeDtypeStruct((I_DEV * rank, late), jnp.float32),
            jax.ShapeDtypeStruct((kgroup, late), jnp.bfloat16),
            jax.ShapeDtypeStruct((rank, kgroup), jnp.float32),
            jax.ShapeDtypeStruct((I_DEV, kgroup), jnp.bfloat16),
        ),
        in_specs=[pl.BlockSpec(memory_space=pltpu.SMEM)] + [pl.BlockSpec(memory_space=pltpu.HBM)] * 4,
        out_specs=(in_vmem,) * 5,
        scratch_shapes=[
            pltpu.VMEM((1, stored), jnp.int32),
            pltpu.VMEM((1, stored), jnp.int32),
            pltpu.VMEM((stored, width), jnp.bfloat16),
            pltpu.VMEM((rank, col_rows), jnp.bfloat16),
            pltpu.VMEM(rows_shape, jnp.bfloat16),
            pltpu.VMEM(meta_shape, jnp.bfloat16),
            pltpu.VMEM(rows_shape, jnp.bfloat16),
            pltpu.VMEM(meta_shape, jnp.bfloat16),
            pltpu.VMEM((I_DEV * rank, width - late), jnp.float32),
            pltpu.SemaphoreType.DMA((sems, members)),
            pltpu.SemaphoreType.DMA((sems, members)),
            pltpu.SemaphoreType.DMA((3,)),
            pltpu.SemaphoreType.DMA((4,)),
            pltpu.SemaphoreType.REGULAR((log2(n) - 1,)),
        ],
        compiler_params=pltpu.CompilerParams(
            collective_id=0, has_side_effects=True, vmem_limit_bytes=24 * 1024 * 1024
        ),
        name="exchange",
    )(
        fiber_count,
        *(
            pltpu.with_memory_space_constraint(x, pltpu.HBM)
            for x in (
                fiber_i.reshape(1, stored),
                fiber_j.reshape(1, stored),
                fiber_rows,
                factor_two.T,
            )
        ),
    )
    return pl.pallas_call(
        functools.partial(finish_kernel, width),
        out_shape=jax.ShapeDtypeStruct((I_DEV, rank * width), jnp.bfloat16),
        in_specs=[in_vmem] * 5,
        out_specs=pl.BlockSpec(memory_space=pl.ANY),
        scratch_shapes=[
            pltpu.VMEM((rank, I_DEV, late), jnp.bfloat16),
            pltpu.SemaphoreType.DMA((2, rank)),
        ],
        compiler_params=pltpu.CompilerParams(vmem_limit_bytes=16 * 1024 * 1024),
        name="finish",
    )(*passed)


def solution(mesh):
    in_specs = (
        P(("row", "col"), None),
        P(("row", "col")),
        P(("row", "col")),
        P(("row", "col")),
        P("col", None),
    )
    out_specs = P(("row", "col"), None)
    step = functools.partial(body, mesh.shape["row"], mesh.shape["col"])
    return jax.shard_map(step, mesh=mesh, in_specs=in_specs, out_specs=out_specs, check_vma=False)
```

```python
import functools

import jax
import jax.numpy as jnp
from jax import lax
from jax.experimental import pallas as pl
from jax.experimental.pallas import tpu as pltpu
from jax.sharding import PartitionSpec as P

I_DEV = 128
LANES = 128
SUBLANES = 8
KBLOCK = 256
GROUPS = 4
LATE = GROUPS - 1
MESH = pl.DeviceIdType.MESH
ORDER = (2, 1, 0)
ARRIVAL = (0, 1, 2)


def log2(x):
    return x.bit_length() - 1


def one_hot(mask):
    return mask.astype(jnp.float32).astype(jnp.bfloat16)


def contract_lanes(a, b):
    return lax.dot_general(a, b, (((1,), (1,)), ((), ())), preferred_element_type=jnp.float32)


def flip(a, b, size):
    out = 0
    bit = 1
    while bit < size:
        out = out + bit * ((a // bit + b // bit) % 2)
        bit *= 2
    return out


def assign_slots(n, cap, count, index):
    stored = index.shape[1]
    live = lax.broadcasted_iota(jnp.int32, (1, stored), 1) < count
    target = jnp.where(live, jnp.right_shift(index, log2(I_DEV)), -1)
    member = lax.broadcasted_iota(jnp.int32, (n, stored), 0) == target
    earlier = lax.broadcasted_iota(jnp.int32, (stored, stored), 0) < lax.broadcasted_iota(
        jnp.int32, (stored, stored), 1
    )
    before = jnp.dot(one_hot(member), one_hot(earlier), preferred_element_type=jnp.float32)
    position = jnp.sum(jnp.where(member, before, 0.0), axis=0, keepdims=True).astype(jnp.int32)
    return target, position


def look_up(local_j, factor_ref):
    rank, col_rows = factor_ref.shape
    stored = local_j.shape[1]
    high = jnp.right_shift(local_j, log2(KBLOCK))
    low = jnp.bitwise_and(local_j, KBLOCK - 1)
    chosen = one_hot(lax.broadcasted_iota(jnp.int32, (KBLOCK, stored), 0) == low)
    pieces = col_rows // KBLOCK
    stacked = jnp.concatenate(
        [factor_ref[:, k * KBLOCK : (k + 1) * KBLOCK] for k in range(pieces)], axis=0
    )
    looked = jnp.dot(stacked, chosen, preferred_element_type=jnp.float32)
    own = jnp.zeros((rank, stored), jnp.float32)
    for k in range(pieces):
        own = own + jnp.where(high == k, looked[k * rank : (k + 1) * rank], 0.0)
    return own


def expand(rank, cap, meta_ref, factor_ref, select_ref):
    members, blocks = meta_ref.shape[:2]
    pack = LANES // cap
    q = rank // pack
    span = members * cap
    held = [
        jnp.concatenate([meta_ref[m, i].astype(jnp.float32) for i in range(blocks - 1)], axis=0)
        for m in range(members)
    ]
    for p in range(pack):
        factor_ref[p * q : (p + 1) * q, :] = jnp.concatenate(
            [block[:q, p * cap : (p + 1) * cap] for block in held], axis=1
        )
    row = jnp.concatenate(
        [meta_ref[m, blocks - 1].astype(jnp.float32)[:1, :cap] for m in range(members)], axis=1
    )
    select_ref[...] = one_hot(
        lax.broadcasted_iota(jnp.int32, (I_DEV, span), 0) == row.astype(jnp.int32)
    )


def spread_factors(select, factor_ref, first, count):
    return jnp.concatenate(
        [
            select * factor_ref[pl.ds(first + b, 1), :].astype(jnp.bfloat16)
            for b in range(count)
        ],
        axis=0,
    )


def exchange_kernel(
    nrow,
    ncol,
    bounds,
    count_ref,
    i_hbm,
    j_hbm,
    fiber_hbm,
    factor_hbm,
    done_ref,
    late_ref,
    late_rows_ref,
    factor_ref,
    select_ref,
    i_ref,
    j_ref,
    fiber_ref,
    own_factor_ref,
    rows_ref,
    meta_ref,
    rrows_ref,
    rmeta_ref,
    total_ref,
    send_sem,
    recv_sem,
    own_sem,
    in_sem,
    known_sem,
):
    n = nrow * ncol
    members, cap, width = rows_ref.shape[1:]
    per = ncol // GROUPS
    parts = len(bounds) - 1
    rank = factor_ref.shape[0]
    stored = fiber_ref.shape[0]
    r = lax.axis_index("row")
    c = lax.axis_index("col")
    z, y = c // per, c % per
    seat = r * per + y

    ready = (
        pltpu.make_async_copy(i_hbm, i_ref, in_sem.at[0]),
        pltpu.make_async_copy(fiber_hbm, fiber_ref, in_sem.at[1]),
        pltpu.make_async_copy(j_hbm, j_ref, in_sem.at[2]),
        pltpu.make_async_copy(factor_hbm, own_factor_ref, in_sem.at[3]),
    )
    sides = [(flip(r, 1 << b, nrow), c) for b in range(log2(nrow))]
    sides += [(r, z * per + flip(y, 1 << b, per)) for b in range(log2(per))]
    low_z = (r, flip(z, 1, GROUPS) * per + y)
    high_z = (r, flip(z, 2, GROUPS) * per + y)
    neighbours = [high_z] + sides + [low_z]
    barrier = pltpu.get_barrier_semaphore()
    for other in neighbours:
        pl.semaphore_signal(barrier, inc=1, device_id=other, device_id_type=MESH)
    for copy in ready:
        copy.start()

    def tell(d):
        other = (sides + [low_z])[d]
        pl.semaphore_signal(known_sem.at[d], inc=1, device_id=other, device_id_type=MESH)

    def hear(d):
        pl.semaphore_wait(known_sem.at[d], 1)

    def partner(g, k):
        return flip(r, k % nrow, nrow), flip(z, g, GROUPS), flip(y, k // nrow, per)

    def remote(g, k, source, dest, row):
        tr, tz, ty = partner(g, k)
        return pltpu.make_async_remote_copy(
            src_ref=source(tr * per + ty),
            dst_ref=dest(seat),
            send_sem=send_sem.at[row, k],
            recv_sem=recv_sem.at[row, k],
            device_id=(tr, tz * per + ty),
            device_id_type=MESH,
        )

    def details(g, k):
        return (
            remote(g, k, lambda t: meta_ref.at[g, t], lambda t: rmeta_ref.at[g, t], g),
        )

    def whole(g, k):
        return (
            remote(
                g, k, lambda t: rows_ref.at[g, t], lambda t: rrows_ref.at[g, t], 2 * GROUPS + g
            ),
        )

    def part(p, k):
        columns = pl.ds(bounds[p], bounds[p + 1] - bounds[p])
        return (
            remote(
                LATE,
                k,
                lambda t: rows_ref.at[LATE, t, :, columns],
                lambda t: rrows_ref.at[LATE, t, :, columns],
                2 * GROUPS + LATE + p,
            ),
        )

    def each(first, copies, act, last=members):
        def step(k, _):
            for copy in copies(k):
                act(copy)
            return 0

        lax.fori_loop(first, last, step, 0)

    def start(copy):
        copy.start()

    own = (
        pltpu.make_async_copy(rows_ref.at[0, seat], rrows_ref.at[0, seat], own_sem.at[0]),
        pltpu.make_async_copy(meta_ref.at[0, seat], rmeta_ref.at[0, seat], own_sem.at[1]),
    )

    ready[0].wait()
    index = i_ref[...]
    target, position = assign_slots(n, cap, count_ref[0], index)
    tcol = jnp.bitwise_and(target, ncol - 1)
    trow = jnp.right_shift(target, log2(ncol))
    tz = jnp.right_shift(tcol, log2(per))
    inner = (trow * per + jnp.bitwise_and(tcol, per - 1)) * cap + position
    inner = jnp.where(target < 0, -1, inner)

    def move_of(g):
        slot = jnp.where(tz == flip(z, g, GROUPS), inner, -1)
        return one_hot(lax.broadcasted_iota(jnp.int32, (members * cap, stored), 0) == slot)

    def pack_rows(g):
        moved = jnp.dot(move_of(g), fiber_ref[...], preferred_element_type=jnp.float32)
        rows_ref[g] = moved.astype(jnp.bfloat16).reshape(members, cap, width)

    ready[1].wait()
    pack_rows(ORDER[0])
    half = members // 2
    pl.semaphore_wait(barrier, len(neighbours))
    tell(0)
    each(0, functools.partial(whole, ORDER[0]), start, 1)
    for d in range(len(sides) - 1):
        hear(d)
        tell(d + 1)
        each(1 << d, functools.partial(whole, ORDER[0]), start, 2 << d)
    pack_rows(ORDER[1])
    hear(len(sides) - 1)
    tell(len(sides))
    pack_rows(ORDER[2])
    hear(len(sides))
    for g in ORDER[1:]:
        each(1 if g == 0 else 0, functools.partial(whole, g), start)
    each(half, functools.partial(whole, ORDER[0]), start)

    ready[2].wait()
    ready[3].wait()
    looked = look_up(j_ref[...] - c * own_factor_ref.shape[1], own_factor_ref)
    local_i = jnp.bitwise_and(index, I_DEV - 1).astype(jnp.float32)
    table = jnp.concatenate(
        [looked, jnp.broadcast_to(local_i, (2 * SUBLANES, stored))], axis=0
    ).astype(jnp.bfloat16)
    pack = LANES // cap
    q = rank // pack
    for g in range(GROUPS):
        spread = contract_lanes(table, move_of(g))
        for m in range(members):
            mine = slice(m * cap, (m + 1) * cap)
            piece = jnp.concatenate(
                [spread[p * q : (p + 1) * q, mine] for p in range(pack)], axis=1
            )
            if q < SUBLANES:
                piece = jnp.concatenate(
                    [piece, jnp.zeros((SUBLANES - q, LANES), jnp.float32)], axis=0
                )
            place = jnp.concatenate(
                [spread[rank : rank + 2, mine], jnp.zeros((2, LANES - cap), jnp.float32)], axis=1
            )
            for i in range(SUBLANES // 2):
                meta_ref[g, m, i] = piece[2 * i : 2 * i + 2].astype(jnp.bfloat16)
            meta_ref[g, m, SUBLANES // 2] = place.astype(jnp.bfloat16)
    for copy in own:
        copy.start()
    for g in ORDER:
        each(1 if g == 0 else 0, functools.partial(details, g), start)
    pack_rows(LATE)
    each(0, functools.partial(part, 0), start)
    each(0, functools.partial(part, 1), start, 2)
    each(0, functools.partial(details, LATE), start)
    each(2, functools.partial(part, 1), start)
    for p in range(2, parts):
        each(0, functools.partial(part, p), start)

    per_step = 8
    span_m = per_step * I_DEV
    kgroup = members * cap

    def rows_of(s):
        return pl.ds(pl.multiple_of(s * span_m, span_m), span_m)

    def arrived(copy):
        copy.wait_recv()

    for order, g in enumerate(ARRIVAL):
        first = 1 if g == 0 else 0
        each(first, functools.partial(whole, g), arrived)
        each(first, functools.partial(details, g), arrived)
        if g == 0:
            for copy in own:
                copy.wait()
        expand(rank, cap, rmeta_ref.at[g], factor_ref, select_ref)

        def multiply(s, _, g=g, order=order):
            left = spread_factors(select_ref[...], factor_ref, s * per_step, per_step)
            product = jnp.dot(
                left, rrows_ref[g].reshape(kgroup, width), preferred_element_type=jnp.float32
            )
            for part_ref, low, high in (
                (total_ref, 0, bounds[-2]),
                (late_ref, bounds[-2], bounds[-1]),
            ):
                term = product[:, low:high]
                if order > 0:
                    term = term + part_ref[rows_of(s), :]
                part_ref[rows_of(s), :] = term
            return 0

        lax.fori_loop(0, rank // per_step, multiply, 0)

    def sent(copy):
        copy.wait_send()

    for g in ORDER:
        each(1 if g == 0 else 0, functools.partial(whole, g), sent)
    for g in range(GROUPS):
        each(1 if g == 0 else 0, functools.partial(details, g), sent)
    each(0, functools.partial(details, LATE), arrived)
    expand(rank, cap, rmeta_ref.at[LATE], factor_ref, select_ref)
    for p in range(parts - 1):
        each(0, functools.partial(part, p), arrived)
        low, high = bounds[p], bounds[p + 1]

        def finish(s, _, low=low, high=high):
            left = spread_factors(select_ref[...], factor_ref, s * per_step, per_step)
            product = jnp.dot(
                left,
                rrows_ref[LATE, :, :, low:high].reshape(kgroup, high - low),
                preferred_element_type=jnp.float32,
            )
            product = (product + total_ref[rows_of(s), low:high]).astype(jnp.bfloat16)
            for b in range(per_step):
                at = pl.multiple_of((s * per_step + b) * width + low, LANES)
                done_ref[:, pl.ds(at, high - low)] = product[b * I_DEV : (b + 1) * I_DEV]
            return 0

        lax.fori_loop(0, rank // per_step, finish, 0)

    for p in range(parts - 1):
        each(0, functools.partial(part, p), sent)
    each(0, functools.partial(part, parts - 1), arrived)
    late_rows_ref[...] = rrows_ref[LATE, :, :, bounds[-2] :].reshape(late_rows_ref.shape)

    for p in range(parts-1,parts):
        each(0, functools.partial(part, p), sent)


def finish_kernel(
    width, done_ref, late_ref, rows_ref, factor_ref, select_ref, out_ref, stage_ref, sem
):
    rank = factor_ref.shape[0]
    late = rows_ref.shape[1]
    early = width - late
    per = 4

    def bulk(b):
        columns = pl.ds(pl.multiple_of(b * width, width), early)
        return pltpu.make_async_copy(done_ref.at[:, columns], out_ref.at[:, columns], sem.at[0, b])

    def rest(b):
        columns = pl.ds(pl.multiple_of(b * width + early, LANES), late)
        return pltpu.make_async_copy(stage_ref.at[b], out_ref.at[:, columns], sem.at[1, b])

    def each(act):
        def step(b, _):
            act(b)
            return 0

        lax.fori_loop(0, rank, step, 0)

    each(lambda b: bulk(b).start())

    def multiply(s, _):
        left = spread_factors(select_ref[...], factor_ref, s * per, per)
        product = jnp.dot(left, rows_ref[...], preferred_element_type=jnp.float32)
        span_m = per * I_DEV
        product = product + late_ref[pl.ds(pl.multiple_of(s * span_m, span_m), span_m), :]
        for b in range(per):
            stage_ref[s * per + b] = product[b * I_DEV : (b + 1) * I_DEV].astype(jnp.bfloat16)
            rest(s * per + b).start()
        return 0

    lax.fori_loop(0, rank // per, multiply, 0)
    each(lambda b: bulk(b).wait())
    each(lambda b: rest(b).wait())


def body(nrow, ncol, fiber_rows, fiber_i, fiber_j, fiber_count, factor_two):
    n = nrow * ncol
    stored, width = fiber_rows.shape
    col_rows, rank = factor_two.shape
    cap = 2 * stored // n
    members = n // GROUPS
    kgroup = members * cap
    bounds = (0, width // 2, width)
    parts = len(bounds) - 1
    late = bounds[-1] - bounds[-2]
    in_vmem = pl.BlockSpec(memory_space=pltpu.VMEM)
    rows_shape = (GROUPS, members, cap, width)
    meta_shape = (GROUPS, members, SUBLANES // 2 + 1, 2, LANES)
    sems = 3 * GROUPS + parts - 1
    passed = pl.pallas_call(
        functools.partial(exchange_kernel, nrow, ncol, bounds),
        out_shape=(
            jax.ShapeDtypeStruct((I_DEV, rank * width), jnp.bfloat16),
            jax.ShapeDtypeStruct((I_DEV * rank, late), jnp.float32),
            jax.ShapeDtypeStruct((kgroup, late), jnp.bfloat16),
            jax.ShapeDtypeStruct((rank, kgroup), jnp.float32),
            jax.ShapeDtypeStruct((I_DEV, kgroup), jnp.bfloat16),
        ),
        in_specs=[pl.BlockSpec(memory_space=pltpu.SMEM)] + [pl.BlockSpec(memory_space=pltpu.HBM)] * 4,
        out_specs=(in_vmem,) * 5,
        scratch_shapes=[
            pltpu.VMEM((1, stored), jnp.int32),
            pltpu.VMEM((1, stored), jnp.int32),
            pltpu.VMEM((stored, width), jnp.bfloat16),
            pltpu.VMEM((rank, col_rows), jnp.bfloat16),
            pltpu.VMEM(rows_shape, jnp.bfloat16),
            pltpu.VMEM(meta_shape, jnp.bfloat16),
            pltpu.VMEM(rows_shape, jnp.bfloat16),
            pltpu.VMEM(meta_shape, jnp.bfloat16),
            pltpu.VMEM((I_DEV * rank, width - late), jnp.float32),
            pltpu.SemaphoreType.DMA((sems, members)),
            pltpu.SemaphoreType.DMA((sems, members)),
            pltpu.SemaphoreType.DMA((3,)),
            pltpu.SemaphoreType.DMA((4,)),
            pltpu.SemaphoreType.REGULAR((log2(n) - 1,)),
        ],
        compiler_params=pltpu.CompilerParams(
            collective_id=0, has_side_effects=True, vmem_limit_bytes=24 * 1024 * 1024
        ),
        name="exchange",
    )(
        fiber_count,
        *(
            pltpu.with_memory_space_constraint(x, pltpu.HBM)
            for x in (
                fiber_i.reshape(1, stored),
                fiber_j.reshape(1, stored),
                fiber_rows,
                factor_two.T,
            )
        ),
    )
    return pl.pallas_call(
        functools.partial(finish_kernel, width),
        out_shape=jax.ShapeDtypeStruct((I_DEV, rank * width), jnp.bfloat16),
        in_specs=[in_vmem] * 5,
        out_specs=pl.BlockSpec(memory_space=pl.ANY),
        scratch_shapes=[
            pltpu.VMEM((rank, I_DEV, late), jnp.bfloat16),
            pltpu.SemaphoreType.DMA((2, rank)),
        ],
        compiler_params=pltpu.CompilerParams(vmem_limit_bytes=16 * 1024 * 1024),
        name="finish",
    )(*passed)


def solution(mesh):
    in_specs = (
        P(("row", "col"), None),
        P(("row", "col")),
        P(("row", "col")),
        P(("row", "col")),
        P("col", None),
    )
    out_specs = P(("row", "col"), None)
    step = functools.partial(body, mesh.shape["row"], mesh.shape["col"])
    return jax.shard_map(step, mesh=mesh, in_specs=in_specs, out_specs=out_specs, check_vma=False)
```
